512 devices in a mesh: ta: 8 (over y, z_hi), ha: 4 (over x), wa: 16 (over z_lo, core).
Axes of the slice: x: 4, y: 4, z: 16 (z_hi: 2, z_lo: 8; z = z_hi * 8 + z_lo), core: 2. Of those that a mesh axis runs over, the one named last changes fastest.
Arguments:
- features: bfloat16 [16, 64, 256, 256], P('ta', 'ha', 'wa'), may hold values from -6 to 6
- conv_weight: bfloat16 [6912, 256], P('wa'), may hold values from -0.078125 to 0.078125
- down_weight: bfloat16 [2, 2, 256, 256], replicated, may hold values from -0.1875 to 0.1875
- grad_out: bfloat16 [16, 32, 128, 256], P('ta', 'ha', 'wa'), may hold values from -6 to 6
- crop_grad: bfloat16 [32768, 8, 8, 256], P(('ta', 'ha', 'wa')), may hold values from -6 to 6
- crop_owner: int32 [32768, 1], P(('ta', 'ha', 'wa')), may hold values from 0 to 63; in each aligned block of 64 rows (0 to 63, 64 to 127, ...) at most 2 rows name the same one
- crop_frame: int32 [32768], P(('ta', 'ha', 'wa')), may hold values from 0 to 1
- crop_row: int32 [32768], P(('ta', 'ha', 'wa')), may hold values from 0 to 8
- crop_col: int32 [32768], P(('ta', 'ha', 'wa')), may hold values from 0 to 8
- crop_valid: int32 [32768], P(('ta', 'ha', 'wa')), may hold values 0 or 1
Outputs:
- reduced: bfloat16 [16, 32, 128, 256], P('ta', 'ha', 'wa')
- grad_in: bfloat16 [16, 64, 256, 256], P('ta', 'ha', 'wa')
The draws below stay inside these ranges and needn't reach their ends.
Inputs may be any that keep to these rules, and one draw needn't show every extreme that they name: `crop_owner`: among one device's 64 crops at most 2 name the same owner, a bound that some block reaches; the owner is the tile of the same time slab whose height index is the value divided by the number of width tiles and whose width index is the remainder. `crop_frame`: frame of the crop within the time slab of the device that holds it. `crop_valid`: padding crops carry gradients that are ignored.
All inputs are finite; a program needn't handle non-finite values. No bound on the sum of `crop_valid` on one device may be relied on, other than what follows from the above.
Results may differ from the reference program's by a relative error of at most 0.0049.
Values may be sent and summed in bfloat16 or wider, within the bound.
A program may use at most 64 MiB of HBM per device.

```python
import math
import jax
import jax.numpy as jnp
import numpy as np
from jax import lax

C = 256
FT = 2
HT = 16
WT = 16
CH = 8
CW = 8
CAP = 2
CROPS_DEV = 64
CROPS = 32768
NF = 16
NH = 64
NW = 256
N_HA = 4
N_WA = 16


def with_ends(array, stream_key, smallest, top_value):
    extent = array.shape
    index_at = [jax.random.randint(jax.random.fold_in(stream_key, axis), (), 0, extent[axis]) for axis in range(len(extent))]
    array = array.at[tuple(index_at)].set(smallest)
    longest = extent.index(max(extent))
    index_at[longest] = (index_at[longest] + 1) % extent[longest]
    return array.at[tuple(index_at)].set(top_value)


def levels(rng, shape, pieces, smallest, high):
    level, own = 1.0, jax.random.fold_in(rng, 6)
    for dim, blocks in pieces:
        steps = jnp.exp(jax.random.uniform(jax.random.fold_in(own, dim), (blocks,), jnp.float32, smallest / len(pieces), high / len(pieces)))
        level = level * jnp.repeat(steps, shape[dim] // blocks).reshape([-1 if axis == dim else 1 for axis in range(len(shape))])
    return level


def routed_block(key, own, number, rows, count, top, reach, slope):
    order = jax.random.permutation(key, count)
    crowded, ordinary = portions_of(count, rows * top, reach, slope, True), portions_of(count, rows * top, reach, slope, False)
    places = jnp.arange(count)

    def named(sizes, rotation):
        used = int((sizes > 0).sum())
        fixed = max(1, used // 4)
        moved = fixed + (places - fixed + rotation * (used - fixed)) % max(1, count - fixed)
        return jnp.zeros((count,), jnp.int32).at[order[jnp.where(places < fixed, places, moved)]].set(jnp.asarray(sizes, jnp.int32))

    sizes = jnp.where(number % 4 == 0, named(crowded, number // 4), named(ordinary, number - number // 4 - 1))
    mixed = jax.random.permutation(jax.random.fold_in(own, 3), count)
    source_of, sink = mixed[0:count // 2 * 2:2], mixed[1:count // 2 * 2:2]
    margin = jnp.minimum(sizes[source_of] - 1, reach - sizes[sink]) // 2
    margin = jnp.where((source_of == order[0]) | (sink == order[0]) | (sizes[sink] == 0), 0, jnp.maximum(margin, 0))
    moved = jax.random.randint(jax.random.fold_in(own, 4), (count // 2,), 0, 1 << 20) % (margin + 1)
    sizes = sizes.at[source_of].add(-moved).at[sink].add(moved)
    labels = jnp.searchsorted(jnp.cumsum(sizes), jnp.arange(rows * top), side="right").astype(jnp.int32)
    table = labels.reshape(top, rows).T
    table = table[jax.random.permutation(jax.random.fold_in(own, 1), rows)]
    rotation = jax.random.randint(jax.random.fold_in(own, 2), (rows, 1), 0, top)
    return jnp.take_along_axis(table, (jnp.arange(top)[None, :] + rotation) % top, axis=1)


def portions_of(number_of, total, reach, lean, full):
    weights = [(1 << 20) // math.isqrt(rank ** lean) + 1 for rank in range(1, number_of + 1)]
    largest = reach if full else min(reach, max(-(-total // number_of), total * weights[0] // sum(weights)))
    least = 1 if total - largest >= number_of - 1 else 0
    counts, surplus = [largest] + [least] * (number_of - 1), total - largest - least * (number_of - 1)
    while surplus > 0:
        candidates = [i for i in range(1, number_of) if counts[i] < largest] or [i for i in range(1, number_of) if counts[i] < reach]
        whole, left = sum([weights[i] for i in candidates]), surplus
        for i in candidates:
            addition = min(reach - counts[i], max(1, left * weights[i] // whole), surplus)
            counts[i] = counts[i] + addition
            surplus = surplus - addition
    return np.array(counts)


def bell_draw(key, dims, scale, most, cuts=(), held_as=jnp.bfloat16):
    level = levels(key, dims, cuts, -0.22, 0.18) if cuts else 1.0
    entries = jax.random.normal(key, dims, jnp.float32) * scale * level
    return jnp.minimum(jnp.maximum(entries, -most), most).astype(held_as)


def setup_inputs(seed: int = 0) -> dict:
    splits = jax.random.split(jax.random.key(seed), 11)
    features = bell_draw(splits[0], (NF, NH, NW, C), 1.0, 6.0, ((0, 8), (1, 4), (2, 16)))
    conv_weight = bell_draw(splits[1], (27 * C, C), (27 * C) ** -0.5, 0.078125, ((0, 16),))
    down_weight = bell_draw(splits[2], (2, 2, C, C), (4 * C) ** -0.5, 0.1875)
    grad_out = bell_draw(splits[3], (NF, NH // 2, NW // 2, C), 1.0, 6.0, ((0, 8), (1, 4), (2, 16)))
    crop_grad = bell_draw(splits[4], (CROPS, CH, CW, C), 1.0, 6.0, ((0, 512),))
    crop_owner_keys = jax.random.split(jax.random.fold_in(splits[5], 1), CROPS // CROPS_DEV)
    crop_owner_turns = jax.random.permutation(jax.random.fold_in(splits[5], 3), CROPS // CROPS_DEV)
    crop_owner = jax.vmap(lambda own, number: routed_block(jax.random.fold_in(splits[5], 2), own, number, CROPS_DEV, N_HA * N_WA, 1, CAP, 2))(crop_owner_keys, crop_owner_turns).reshape((CROPS, 1))
    crop_frame = with_ends(jax.random.randint(splits[6], (CROPS,), 0, FT), jax.random.fold_in(splits[6], 1), 0, FT - 1).astype(jnp.int32)
    crop_row = with_ends(jax.random.randint(splits[7], (CROPS,), 0, HT - CH + 1), jax.random.fold_in(splits[7], 1), 0, HT - CH).astype(jnp.int32)
    crop_col = with_ends(jax.random.randint(splits[8], (CROPS,), 0, WT - CW + 1), jax.random.fold_in(splits[8], 1), 0, WT - CW).astype(jnp.int32)
    crop_valid = with_ends((jax.random.randint(splits[9], (CROPS,), 0, 4) < 3).astype(jnp.int32), jax.random.fold_in(splits[9], 1), 0, 1)
    return {"features": features, "conv_weight": conv_weight, "down_weight": down_weight, "grad_out": grad_out, "crop_grad": crop_grad, "crop_owner": crop_owner, "crop_frame": crop_frame, "crop_row": crop_row, "crop_col": crop_col, "crop_valid": crop_valid}


def convolve(padded, kernel_taps, frames, rows, cols):
    width = kernel_taps.shape[-1]

    def one_frame(first_frame):
        window = lax.dynamic_slice_in_dim(padded, first_frame, 3, 0)
        summed = jnp.zeros((rows * cols, width), jnp.float32)
        for frame_off in range(3):
            for row_off in range(3):
                for col_off in range(3):
                    shifted = window[frame_off, row_off:row_off + rows, col_off:col_off + cols, :].reshape(rows * cols, width)
                    summed = summed + jnp.dot(shifted, kernel_taps[(frame_off * 3 + row_off) * 3 + col_off], preferred_element_type=jnp.float32)
        return summed.reshape(rows, cols, width)

    return lax.map(one_frame, jnp.arange(frames).astype(jnp.int32))


def reference(features, conv_weight, down_weight, grad_out, crop_grad, crop_owner, crop_frame, crop_row, crop_col, crop_valid):
    kernel_taps = conv_weight.reshape(27, C, C)
    padded = jnp.pad(features, ((2, 0), (1, 1), (1, 1), (0, 0)))
    preact = convolve(padded, kernel_taps, NF, NH, NW)
    sigmoid_h = jax.nn.sigmoid(preact)
    section_out = (features.astype(jnp.float32) + preact * sigmoid_h).astype(jnp.bfloat16)
    down_mat = down_weight.reshape(4 * C, C)
    pooled = section_out.reshape(NF, NH // 2, 2, NW // 2, 2, C).transpose(0, 1, 3, 2, 4, 5).reshape(-1, 4 * C)
    reduced = jnp.dot(pooled, down_mat, preferred_element_type=jnp.float32).astype(jnp.bfloat16).reshape(NF, NH // 2, NW // 2, C)
    spread = jnp.dot(grad_out.reshape(-1, C), down_mat.T, preferred_element_type=jnp.float32)
    spread = spread.reshape(NF, NH // 2, NW // 2, 2, 2, C).transpose(0, 1, 3, 2, 4, 5).reshape(NF, NH, NW, C)
    grad_pre = (spread * sigmoid_h * (1.0 + preact * (1.0 - sigmoid_h))).astype(jnp.bfloat16)
    flipped = jnp.transpose(kernel_taps[::-1], (0, 2, 1))
    back_pad = jnp.pad(grad_pre, ((0, 2), (1, 1), (1, 1), (0, 0)))
    through = convolve(back_pad, flipped, NF, NH, NW)
    crop_number = jnp.arange(CROPS).astype(jnp.int32)
    time_slab = crop_number // (CROPS_DEV * N_HA * N_WA)
    owner_id = crop_owner[:, 0]
    frame_at = time_slab * FT + crop_frame
    first_row = (owner_id // N_WA) * HT + crop_row
    first_col = (owner_id % N_WA) * WT + crop_col
    row_steps = jnp.arange(CH).astype(jnp.int32)
    col_steps = jnp.arange(CW).astype(jnp.int32)
    cell_index = (frame_at[:, None, None] * NH + first_row[:, None, None] + row_steps[None, :, None]) * NW + first_col[:, None, None] + col_steps[None, None, :]
    crop_values = crop_grad.astype(jnp.float32) * crop_valid.astype(jnp.float32)[:, None, None, None]
    crop_terms = jnp.zeros((NF * NH * NW, C), jnp.float32).at[cell_index.reshape(-1)].add(crop_values.reshape(-1, C))
    grad_in = (spread + through + crop_terms.reshape(NF, NH, NW, C)).astype(jnp.bfloat16)
    return reduced, grad_in
```

```python
import functools

import jax
import jax.numpy as jnp
from jax import lax
from jax.experimental import pallas as pl
from jax.experimental.pallas import tpu as pltpu
from jax.sharding import PartitionSpec as P

MESH = pl.DeviceIdType.MESH
CAP = 2


def place():
    slab, x, strip = lax.axis_index("ta"), lax.axis_index("ha"), lax.axis_index("wa")
    return slab // 2, (slab % 2) * 8 + strip // 2, x, strip % 2


def at(y, z, x, core):
    y, z, x = (y + 4) % 4, (z + 16) % 16, (x + 4) % 4
    return (y * 2 + z // 8, x, (z % 8) * 2 + core)


class Copies:
    def __init__(self, send_sems, recv_sems):
        self.send_sems, self.recv_sems, self.used, self.sent = send_sems, recv_sems, 0, []

    def make(self, src, dst, device):
        slot = self.used
        self.used += 1
        return pltpu.make_async_remote_copy(
            src_ref=src,
            dst_ref=dst,
            send_sem=self.send_sems.at[slot],
            recv_sem=self.recv_sems.at[slot],
            device_id=device,
            device_id_type=MESH,
        )

    def start(self, src, dst, device):
        copy = self.make(src, dst, device)
        copy.start()
        self.sent.append(copy)
        return copy


def greet(devices):
    barrier = pltpu.get_barrier_semaphore()
    for device in devices:
        pl.semaphore_signal(barrier, inc=1, device_id=device, device_id_type=MESH)
    pl.semaphore_wait(barrier, len(devices))


def edge_columns(ext, edge, frame):
    rows, cols, width = ext.shape[1:]
    flat = ext[frame].reshape(rows * cols, width)
    row = lax.broadcasted_iota(jnp.int32, (edge.shape[2], rows * cols), 0)
    cell = lax.broadcasted_iota(jnp.int32, (edge.shape[2], rows * cols), 1)
    for side, col in ((0, 0), (1, cols - 1)):
        pick = jnp.where(cell == row * cols + col, 1.0, 0.0).astype(jnp.bfloat16)
        edge[side, frame] = jnp.dot(pick, flat, preferred_element_type=jnp.float32).astype(
            jnp.bfloat16
        )


class Halo:
    def __init__(self, copies, tile, ext, left, right, relay, edge, own, other, step):
        self.copies, self.tile, self.ext, self.left, self.right = copies, tile, ext, left, right
        self.relay, self.edge, self.own, self.other, self.step = relay, edge, own, other, step

    def first(self):
        y, z, x, core = place()
        self.up = self.copies.start(self.tile.at[0], self.relay.at[0], at(y, z + 4, x, core))
        self.down = self.copies.start(self.tile.at[1], self.relay.at[1], at(y, z - 4, x, core))

    def own_rows(self):
        y, z, x, core = place()
        ext, own = self.ext, self.own
        rows = self.tile.shape[1]
        self.rows_own = [
            self.copies.start(
                self.tile.at[:, pl.ds(rows - 1, 1)],
                ext.at[pl.ds(own, 2), pl.ds(0, 1)],
                at(y, z, x + 1, core),
            ),
            self.copies.start(
                self.tile.at[:, pl.ds(0, 1)],
                ext.at[pl.ds(own, 2), pl.ds(rows + 1, 1)],
                at(y, z, x - 1, core),
            ),
        ]
        ext[own : own + 2, 1 : rows + 1] = self.tile[...]

    def forward(self):
        y, z, x, core = place()
        rows = self.tile.shape[1]
        self.far = []
        for frame, copy, turn in ((0, self.up, 4), (1, self.down, -4)):
            source_hi = ((z - turn + 16) % 16) // 8
            y_to = y + source_hi if self.step == 1 else y - 1 + source_hi
            copy.wait_recv()
            self.far.append(
                self.copies.start(
                    self.relay.at[frame],
                    self.ext.at[self.other + frame, pl.ds(1, rows)],
                    at(y_to, z + turn, x, core),
                )
            )

    def finish(self):
        y, z, x, core = place()
        ext, other = self.ext, self.other
        rows = self.tile.shape[1]
        for copy in self.rows_own:
            copy.wait_recv()
        for frame in range(2):
            edge_columns(ext, self.edge, self.own + frame)
        for copy in self.far:
            copy.wait_recv()
        borders = [
            self.copies.start(
                ext.at[pl.ds(other, 2), pl.ds(rows, 1)],
                ext.at[pl.ds(other, 2), pl.ds(0, 1)],
                at(y, z, x + 1, core),
            ),
            self.copies.start(
                ext.at[pl.ds(other, 2), pl.ds(1, 1)],
                ext.at[pl.ds(other, 2), pl.ds(rows + 1, 1)],
                at(y, z, x - 1, core),
            ),
        ]
        for copy in borders:
            copy.wait_recv()
        for frame in range(2):
            edge_columns(ext, self.edge, other + frame)
        sides = [
            self.copies.start(self.edge.at[1], self.left, at(y, z + core, x, 1 - core)),
            self.copies.start(self.edge.at[0], self.right, at(y, z - 1 + core, x, 1 - core)),
        ]
        for copy in sides:
            copy.wait_recv()


def halo_partners():
    y, z, x, core = place()
    return [
        at(y, z + 4, x, core),
        at(y, z - 4, x, core),
        at(y + 1, z + 4, x, core),
        at(y - 1, z - 4, x, core),
        at(y + 1, z - 4, x, core),
        at(y - 1, z + 4, x, core),
        at(y, z, x + 1, core),
        at(y, z, x - 1, core),
        at(y, z, x, 1 - core),
        at(y, z + 1, x, core),
        at(y, z - 1, x, core),
        at(y, z - 1 + 2 * core, x, 1 - core),
    ]


def gather_kernel(
    tile, shard, packed, cells, ext, left, right, taps, crops, places,
    relay, edge, cross, keep, send_sems, recv_sems, local_sems,
):
    y, z, x, core = place()
    strip = z % 8
    copies = Copies(send_sems, recv_sems)
    greet(
        halo_partners()
        + [
            at(y, z, x + 1, 1 - core),
            at(y, z, x - 1, 1 - core),
            at(y, z, x + 2, core),
            at(y, z, x + 2, 1 - core),
            at(y + 1, z, x, core),
            at(y - 1, z, x, core),
        ]
    )
    halo = Halo(copies, tile, ext, left, right, relay, edge, 2, 0, 1)
    half = pl.ds(pl.multiple_of((y % 2) * 128, 128), 128)
    mine = x * 2 + core
    turn = 1 - 2 * core

    def lane(offset):
        return ((strip + offset + 8) % 8) * 2 + core

    across = (x + 2) % 4
    cross_in = [
        copies.start(
            packed.at[across * 2 + (core + flip) % 2],
            cross.at[flip],
            at(y, z, x + turn, core),
        )
        for flip in range(2)
    ]
    halo.first()
    ring = {}
    for way in (1, -1):
        ring[way] = copies.start(
            shard.at[:, half], taps.at[lane(0), :, half], at(y, z + way, x, core)
        )
    halo.own_rows()
    got = []
    for away in (1, -1):
        for flip in range(2):
            to = (core + flip) % 2
            got.append(
                copies.start(
                    packed.at[((x + away + 4) % 4) * 2 + to],
                    crops.at[:, mine],
                    at(y, z, x + away, to),
                )
            )
    got.append(
        copies.start(packed.at[x * 2 + 1 - core], crops.at[:, mine], at(y, z, x, 1 - core))
    )
    for away in (1, 2, 3):
        for flip in range(2):
            to = (core + flip) % 2
            got.append(
                copies.start(
                    cells.at[((x + away) % 4) * 2 + to], places.at[mine], at(y, z, x + away, to)
                )
            )
    got.append(
        copies.start(cells.at[x * 2 + 1 - core], places.at[mine], at(y, z, x, 1 - core))
    )
    got.append(copies.start(shard, taps.at[lane(0)], at(y, z, x, 1 - core)))
    own_shard = pltpu.make_async_copy(shard, taps.at[lane(0)], local_sems.at[0])
    own_shard.start()
    own_in = pltpu.make_async_copy(packed.at[mine], keep, local_sems.at[1])
    own_in.start()
    places[mine] = cells[mine]

    swaps = {}

    def swap(offset, y_to):
        piece = taps.at[lane(offset), :, half]
        swaps[offset] = copies.start(piece, piece, at(y_to, z, x, core))

    def ring_step(step):
        for way in (1, -1):
            ring[way].wait_recv()
            offset = -way * step
            if step < 3:
                piece = taps.at[lane(offset), :, half]
                ring[way] = copies.start(piece, piece, at(y, z + way, x, core))
            swap(offset, y + way)

    ring_step(1)
    ring_step(2)
    own_in.wait()
    own_out = pltpu.make_async_copy(keep, crops.at[:, mine], local_sems.at[2])
    own_out.start()

    def cross_out(flip):
        cross_in[flip].wait_recv()
        source = ((x - turn + 4) % 4) * 2 + core
        got.append(
            copies.start(
                cross.at[flip],
                crops.at[:, source],
                at(y, z, x + turn, (core + flip) % 2),
            )
        )

    ring_step(3)
    last = taps.at[lane(4), :, half]
    piece = taps.at[lane(-3 * turn), :, half]
    ring_last = copies.start(piece, piece, at(y, z + turn, x, core))
    cross_out(0)
    halo.forward()
    cross_out(1)
    ring_last.wait_recv()
    swaps[4] = copies.start(last, last, at(y + turn, z, x, core))
    for offset in (1, -1, 2, -2, 3, -3, 4):
        swaps[offset].wait_recv()
        whole = taps.at[lane(offset)]
        got.append(copies.start(whole, whole, at(y, z, x, 1 - core)))
    halo.finish()
    assert copies.used == 48, copies.used
    for copy in got:
        copy.wait_recv()
    own_shard.wait()
    own_out.wait()
    for copy in copies.sent:
        copy.wait_send()


def scatter_kernel(
    tile, part, ext, left, right, total,
    relay, edge, in_up, in_down, out_up, out_down,
    send_sems, recv_sems, up_send, up_recv, down_send, down_recv,
):
    y, z, x, core = place()
    strip = z % 8
    copies = Copies(send_sems, recv_sems)
    greet(halo_partners())
    halo = Halo(copies, tile, ext, left, right, relay, edge, 0, 2, -1)
    halo.first()
    halo.own_rows()

    def chain(goal, chunk, way):
        landing, leaving, sends, recvs = (
            (in_up, out_up, up_send, up_recv) if way == 1 else (in_down, out_down, down_send, down_recv)
        )
        return pltpu.make_async_remote_copy(
            src_ref=leaving.at[goal, chunk],
            dst_ref=landing.at[goal, chunk],
            send_sem=sends.at[goal, chunk],
            recv_sem=recvs.at[goal, chunk],
            device_id=at(y, z + way, x, core),
            device_id_type=MESH,
        )

    def advance(step, chunk, way):
        rank = strip if way == 1 else 7 - strip
        ahead = 7 - step + rank

        @pl.when(rank <= step)
        def _():
            goal = ahead if way == 1 else 7 - ahead
            copy = chain(goal, chunk, way)
            landing, leaving = (in_up, out_up) if way == 1 else (in_down, out_down)

            @pl.when(rank > 0)
            def _():
                copy.wait_recv()
                summed = part[goal, chunk].astype(jnp.float32) + landing[goal, chunk].astype(
                    jnp.float32
                )
                leaving[goal, chunk] = summed.astype(jnp.bfloat16)

            @pl.when(rank == 0)
            def _():
                leaving[goal, chunk] = part[goal, chunk]

            copy.start()

    for step in range(7):
        for chunk in range(2):
            for way in (1, -1):
                advance(step, chunk, way)
        if step == 3:
            halo.forward()
    halo.finish()
    for chunk in range(2):
        total[chunk] = part[strip, chunk].astype(jnp.float32)
        for way in (1, -1):
            landing = in_up if way == 1 else in_down

            @pl.when((strip if way == 1 else 7 - strip) > 0)
            def _():
                chain(strip, chunk, way).wait_recv()
                total[chunk] += landing[strip, chunk].astype(jnp.float32)

    for step in range(7):
        for chunk in range(2):
            for way in (1, -1):
                rank = strip if way == 1 else 7 - strip

                @pl.when(rank <= step)
                def _():
                    ahead = 7 - step + rank
                    chain(ahead if way == 1 else 7 - ahead, chunk, way).wait_send()

    for copy in copies.sent:
        copy.wait_send()


def pack_kernel(owner, frame, row, col, valid, crop, packed, cells, count, base):
    packed[...] = jnp.zeros_like(packed)

    def clear(i, _):
        count[i] = 0
        base[2 * i] = 0
        base[2 * i + 1] = 0
        return 0

    lax.fori_loop(0, 64, clear, 0)

    def put(k, _):
        @pl.when(valid[k] != 0)
        def _():
            name = owner[k]
            rank = count[name]
            count[name] = rank + 1
            slot = ((name // 16) * 2 + name % 2) * 16 + (name % 16) // 2 * 2 + rank
            base[slot] = frame[k] * 256 + row[k] * 16 + col[k]
            packed[slot] = crop[k]

        return 0

    lax.fori_loop(0, 64, put, 0)
    where = lax.broadcasted_iota(jnp.int32, (1, 128), 1)
    offset = (where % 64) // 8 * 16 + where % 8

    def mark(i, _):
        cells[pl.ds(i, 1), :] = offset + jnp.where(where < 64, base[2 * i], base[2 * i + 1])
        return 0

    lax.fori_loop(0, 64, mark, 0)


def place_kernel(crops, places, part):
    goal = pl.program_id(0)
    cell = lax.broadcasted_iota(jnp.int32, (512, 128), 0)
    summed = jnp.zeros((512, 256), jnp.float32)
    for pair in range(4):
        hits = [
            jnp.where(cell == places[2 * pair + i, pl.ds(goal, 1), :], 1.0, 0.0).astype(jnp.bfloat16)
            for i in range(2)
        ]
        summed += jnp.dot(
            jnp.concatenate(hits, 1),
            crops[0, 2 * pair : 2 * pair + 2].reshape(256, 256),
            preferred_element_type=jnp.float32,
        )
    part[0] = summed.astype(jnp.bfloat16)


def convolve(padded, kernel_taps, frames, rows, cols):
    width = kernel_taps.shape[-1]
    summed = jnp.zeros((frames * rows * cols, width), jnp.float32)
    for frame_off in range(3):
        windows = []
        for row_off in range(3):
            for col_off in range(3):
                windows.append(
                    padded[
                        frame_off : frame_off + frames,
                        row_off : row_off + rows,
                        col_off : col_off + cols,
                        :,
                    ]
                )
        stacked = jnp.concatenate(windows, -1).reshape(frames * rows * cols, 9 * width)
        tap_block = kernel_taps[frame_off * 9 : (frame_off + 1) * 9].reshape(9 * width, width)
        summed = summed + jnp.dot(stacked, tap_block, preferred_element_type=jnp.float32)
    return summed.reshape(frames, rows, cols, width)


def joined(ext, left, right, far_frames, far_there):
    rows = ext.shape[1]
    x, strip = lax.axis_index("ha"), lax.axis_index("wa")
    frame = lax.broadcasted_iota(jnp.int32, (4, rows, 1, 1), 0)
    row = lax.broadcasted_iota(jnp.int32, (4, rows, 1, 1), 1)
    there = (
        ((row > 0) | (x > 0))
        & ((row < rows - 1) | (x < 3))
        & (((frame < far_frames[0]) | (frame > far_frames[1])) | far_there)
    )
    zero = jnp.zeros((), jnp.bfloat16)
    padded = jnp.concatenate(
        [
            jnp.where(strip > 0, left[:, :rows, None, :], zero),
            ext,
            jnp.where(strip < 15, right[:, :rows, None, :], zero),
        ],
        2,
    )
    return jnp.where(there, padded, zero)


VM = functools.partial(pl.BlockSpec, memory_space=pltpu.VMEM)
SM = functools.partial(pl.BlockSpec, memory_space=pltpu.SMEM)
ANY = functools.partial(pl.BlockSpec, memory_space=pl.ANY)
DMA = pltpu.SemaphoreType.DMA


def per_device(
    features, conv_weight, down_weight, grad_out, crop_grad,
    crop_owner, crop_frame, crop_row, crop_col, crop_valid,
):
    frames, rows, cols, width = features.shape
    half_type, shape = jnp.bfloat16, jax.ShapeDtypeStruct
    packed, cells = pl.pallas_call(
        pack_kernel,
        out_shape=(shape((128, 64, width), half_type), shape((64, 128), jnp.int32)),
        in_specs=[SM()] * 5 + [VM()],
        out_specs=(VM(), VM()),
        scratch_shapes=[pltpu.SMEM((64,), jnp.int32), pltpu.SMEM((128,), jnp.int32)],
        compiler_params=pltpu.CompilerParams(vmem_limit_bytes=32 << 20),
    )(
        crop_owner[:, 0], crop_frame, crop_row, crop_col, crop_valid,
        crop_grad.reshape(64, 64, width),
    )
    ext_shape = shape((4, rows + 2, cols, width), half_type)
    side_shape = shape((4, 32, width), half_type)
    copies_a, copies_b = 48, 10
    ext, left, right, taps, crops, places = pl.pallas_call(
        gather_kernel,
        out_shape=(
            ext_shape, side_shape, side_shape,
            shape((16, 432, width), half_type),
            shape((8, 8, 128, width), half_type),
            shape((8, 8, 128), jnp.int32),
        ),
        in_specs=[VM(), VM(), ANY(), VM()],
        out_specs=(VM(), VM(), VM(), ANY(), ANY(), VM()),
        scratch_shapes=[
            pltpu.VMEM((2, rows, cols, width), half_type),
            pltpu.VMEM((2, 4, 32, width), half_type),
            pltpu.VMEM((2, 8, 128, width), half_type),
            pltpu.VMEM((8, 128, width), half_type),
            DMA((copies_a,)), DMA((copies_a,)), DMA((3,)),
        ],
        compiler_params=pltpu.CompilerParams(
            collective_id=0, has_side_effects=True, vmem_limit_bytes=32 << 20
        ),
    )(features, conv_weight, packed.reshape(8, 8, 128, width), cells.reshape(8, 8, 128))
    part = pl.pallas_call(
        place_kernel,
        grid=(8,),
        out_shape=shape((8, 512, width), half_type),
        in_specs=[pl.BlockSpec((1, 8, 128, width), lambda i: (i, 0, 0, 0)), VM()],
        out_specs=pl.BlockSpec((1, 512, width), lambda i: (i, 0, 0)),
    )(crops, places)
    slab = lax.axis_index("ta")
    kernel_taps = taps.reshape(27, width, width)
    padded = joined(ext, left, right, (0, 1), slab > 0)
    preact = convolve(padded, kernel_taps, frames, rows, cols)
    sigmoid_h = jax.nn.sigmoid(preact)
    section_out = (features.astype(jnp.float32) + preact * sigmoid_h).astype(jnp.bfloat16)
    down_mat = down_weight.reshape(4 * width, width)
    pooled = (
        section_out.reshape(frames, rows // 2, 2, cols // 2, 2, width)
        .transpose(0, 1, 3, 2, 4, 5)
        .reshape(-1, 4 * width)
    )
    reduced = (
        jnp.dot(pooled, down_mat, preferred_element_type=jnp.float32)
        .astype(jnp.bfloat16)
        .reshape(frames, rows // 2, cols // 2, width)
    )
    spread = jnp.dot(grad_out.reshape(-1, width), down_mat.T, preferred_element_type=jnp.float32)
    spread = (
        spread.reshape(frames, rows // 2, cols // 2, 2, 2, width)
        .transpose(0, 1, 3, 2, 4, 5)
        .reshape(frames, rows, cols, width)
    )
    grad_pre = (spread * sigmoid_h * (1.0 + preact * (1.0 - sigmoid_h))).astype(jnp.bfloat16)
    chain = pltpu.VMEM((8, 2, 256, width), half_type)
    ext, left, right, crop_terms = pl.pallas_call(
        scatter_kernel,
        out_shape=(
            ext_shape, side_shape, side_shape, shape((2, 256, width), jnp.float32),
        ),
        in_specs=[VM(), VM()],
        out_specs=(VM(), VM(), VM(), VM()),
        scratch_shapes=[
            pltpu.VMEM((2, rows, cols, width), half_type),
            pltpu.VMEM((2, 4, 32, width), half_type),
            chain, chain, chain, chain,
            DMA((copies_b,)), DMA((copies_b,)),
            DMA((8, 2)), DMA((8, 2)), DMA((8, 2)), DMA((8, 2)),
        ],
        compiler_params=pltpu.CompilerParams(
            collective_id=1, has_side_effects=True, vmem_limit_bytes=32 << 20
        ),
    )(grad_pre, part.reshape(8, 2, 256, width))
    flipped = jnp.transpose(kernel_taps[::-1], (0, 2, 1))
    back_pad = joined(ext, left, right, (2, 3), slab < 7)
    through = convolve(back_pad, flipped, frames, rows, cols)
    grad_in = (spread + through + crop_terms.reshape(frames, rows, cols, width)).astype(
        jnp.bfloat16
    )
    return (reduced, grad_in)


def solution(mesh):
    spread_all = ("ta", "ha", "wa")
    tile = P("ta", "ha", "wa", None)
    in_specs = (
        tile, P("wa", None), P(), tile, P(spread_all, None, None, None), P(spread_all, None),
        P(spread_all), P(spread_all), P(spread_all), P(spread_all),
    )
    return jax.shard_map(
        per_device, mesh=mesh, in_specs=in_specs, out_specs=(tile, tile), check_vma=False
    )
```

```python
import functools

import jax
import jax.numpy as jnp
from jax import lax
from jax.experimental import pallas as pl
from jax.experimental.pallas import tpu as pltpu
from jax.sharding import PartitionSpec as P

MESH = pl.DeviceIdType.MESH
CAP = 2


def place():
    slab, x, strip = lax.axis_index("ta"), lax.axis_index("ha"), lax.axis_index("wa")
    return slab // 2, (slab % 2) * 8 + strip // 2, x, strip % 2


def at(y, z, x, core):
    y, z, x = (y + 4) % 4, (z + 16) % 16, (x + 4) % 4
    return (y * 2 + z // 8, x, (z % 8) * 2 + core)


class Copies:
    def __init__(self, send_sems, recv_sems):
        self.send_sems, self.recv_sems, self.used, self.sent = send_sems, recv_sems, 0, []

    def make(self, src, dst, device):
        slot = self.used
        self.used += 1
        return pltpu.make_async_remote_copy(
            src_ref=src,
            dst_ref=dst,
            send_sem=self.send_sems.at[slot],
            recv_sem=self.recv_sems.at[slot],
            device_id=device,
            device_id_type=MESH,
        )

    def start(self, src, dst, device):
        copy = self.make(src, dst, device)
        copy.start()
        self.sent.append(copy)
        return copy


def greet(devices):
    barrier = pltpu.get_barrier_semaphore()
    for device in devices:
        pl.semaphore_signal(barrier, inc=1, device_id=device, device_id_type=MESH)
    pl.semaphore_wait(barrier, len(devices))


def edge_columns(ext, edge, frame):
    rows, cols, width = ext.shape[1:]
    flat = ext[frame].reshape(rows * cols, width)
    row = lax.broadcasted_iota(jnp.int32, (edge.shape[2], rows * cols), 0)
    cell = lax.broadcasted_iota(jnp.int32, (edge.shape[2], rows * cols), 1)
    for side, col in ((0, 0), (1, cols - 1)):
        pick = jnp.where(cell == row * cols + col, 1.0, 0.0).astype(jnp.bfloat16)
        edge[side, frame] = jnp.dot(pick, flat, preferred_element_type=jnp.float32).astype(
            jnp.bfloat16
        )


class Halo:
    def __init__(self, copies, tile, ext, left, right, relay, edge, own, other, step):
        self.copies, self.tile, self.ext, self.left, self.right = copies, tile, ext, left, right
        self.relay, self.edge, self.own, self.other, self.step = relay, edge, own, other, step

    def first(self):
        y, z, x, core = place()
        self.up = self.copies.start(self.tile.at[0], self.relay.at[0], at(y, z + 4, x, core))
        self.down = self.copies.start(self.tile.at[1], self.relay.at[1], at(y, z - 4, x, core))

    def own_rows(self):
        y, z, x, core = place()
        ext, own = self.ext, self.own
        rows = self.tile.shape[1]
        self.rows_own = [
            self.copies.start(
                self.tile.at[:, pl.ds(rows - 1, 1)],
                ext.at[pl.ds(own, 2), pl.ds(0, 1)],
                at(y, z, x + 1, core),
            ),
            self.copies.start(
                self.tile.at[:, pl.ds(0, 1)],
                ext.at[pl.ds(own, 2), pl.ds(rows + 1, 1)],
                at(y, z, x - 1, core),
            ),
        ]
        ext[own : own + 2, 1 : rows + 1] = self.tile[...]

    def forward(self):
        y, z, x, core = place()
        rows = self.tile.shape[1]
        self.far = []
        for frame, copy, turn in ((0, self.up, 4), (1, self.down, -4)):
            source_hi = ((z - turn + 16) % 16) // 8
            y_to = y + source_hi if self.step == 1 else y - 1 + source_hi
            copy.wait_recv()
            self.far.append(
                self.copies.start(
                    self.relay.at[frame],
                    self.ext.at[self.other + frame, pl.ds(1, rows)],
                    at(y_to, z + turn, x, core),
                )
            )

    def near_columns(self):
        for copy in self.rows_own:
            copy.wait_recv()
        for frame in range(2):
            edge_columns(self.ext, self.edge, self.own + frame)

    def far_rows(self):
        y, z, x, core = place()
        ext, other = self.ext, self.other
        rows = self.tile.shape[1]
        for copy in self.far:
            copy.wait_recv()
        self.borders = [
            self.copies.start(
                ext.at[pl.ds(other, 2), pl.ds(rows, 1)],
                ext.at[pl.ds(other, 2), pl.ds(0, 1)],
                at(y, z, x + 1, core),
            ),
            self.copies.start(
                ext.at[pl.ds(other, 2), pl.ds(1, 1)],
                ext.at[pl.ds(other, 2), pl.ds(rows + 1, 1)],
                at(y, z, x - 1, core),
            ),
        ]

    def finish(self):
        y, z, x, core = place()
        for copy in self.borders:
            copy.wait_recv()
        for frame in range(2):
            edge_columns(self.ext, self.edge, self.other + frame)
        sides = [
            self.copies.start(self.edge.at[1], self.left, at(y, z + core, x, 1 - core)),
            self.copies.start(self.edge.at[0], self.right, at(y, z - 1 + core, x, 1 - core)),
        ]
        for copy in sides:
            copy.wait_recv()


def halo_partners():
    y, z, x, core = place()
    return [
        at(y, z + 4, x, core),
        at(y, z - 4, x, core),
        at(y + 1, z + 4, x, core),
        at(y - 1, z - 4, x, core),
        at(y + 1, z - 4, x, core),
        at(y - 1, z + 4, x, core),
        at(y, z, x + 1, core),
        at(y, z, x - 1, core),
        at(y, z, x, 1 - core),
        at(y, z + 1, x, core),
        at(y, z - 1, x, core),
        at(y, z - 1 + 2 * core, x, 1 - core),
    ]


def table_kernel(owner, frame, row, col, valid, source, cells, index, count, base, sems):
    moves = [
        pltpu.make_async_copy(ref, index.at[i], sems.at[i])
        for i, ref in enumerate((owner, frame, row, col, valid))
    ]
    for move in moves:
        move.start()

    def clear(i, _):
        count[i] = 0
        for rank in range(2):
            base[2 * i + rank] = 0
            source[2 * i + rank] = 64
        return 0

    lax.fori_loop(0, 64, clear, 0)
    for move in moves:
        move.wait()

    def put(k, _):
        @pl.when(index[4, k] != 0)
        def _():
            name = index[0, k]
            rank = count[name]
            count[name] = rank + 1
            deep = (name % 16) // 2
            spot = jnp.where(deep < 4, 2 * deep + 1, 2 * (7 - deep))
            slot = ((name // 16) * 2 + name % 2) * 16 + spot * 2 + rank
            base[slot] = index[1, k] * 256 + index[2, k] * 16 + index[3, k]
            source[slot] = k

        return 0

    lax.fori_loop(0, 64, put, 0)
    where = lax.broadcasted_iota(jnp.int32, (1, 128), 1)
    offset = (where % 64) // 8 * 16 + where % 8

    def mark(i, _):
        cells[pl.ds(i, 1), :] = offset + jnp.where(where < 64, base[2 * i], base[2 * i + 1])
        return 0

    lax.fori_loop(0, 64, mark, 0)


def gather_kernel(
    tile, shard, source, cells, crop_grad, ext, left, right, taps, total,
    relay, edge, crop, packed, crops, places, cross, part,
    in_up, in_down, out_up, out_down,
    send_sems, recv_sems, local_sems, up_send, up_recv, down_send, down_recv,
):
    y, z, x, core = place()
    strip = z % 8
    copies = Copies(send_sems, recv_sems)
    crop_in = pltpu.make_async_copy(crop_grad, crop.at[pl.ds(0, 64)], local_sems.at[1])
    crop_in.start()
    own_shard = pltpu.make_async_copy(shard, taps.at[strip * 2 + core], local_sems.at[0])
    own_shard.start()
    crop[64] = jnp.zeros_like(crop[64])
    greet(
        halo_partners()
        + [
            at(y, z, x + 1, 1 - core),
            at(y, z, x - 1, 1 - core),
            at(y, z, x + 2, core),
            at(y, z, x + 2, 1 - core),
            at(y + 1, z, x, core),
            at(y - 1, z, x, core),
        ]
    )
    halo = Halo(copies, tile, ext, left, right, relay, edge, 2, 0, 1)
    half = pl.ds(pl.multiple_of((y % 2) * 128, 128), 128)
    mine = x * 2 + core
    turn = 1 - 2 * core

    def lane(offset):
        return ((strip + offset + 8) % 8) * 2 + core

    ring = {}
    for way in (1, -1):
        ring[way] = copies.start(
            shard.at[:, half], taps.at[lane(0), :, half], at(y, z + way, x, core)
        )
    crop_in.wait()

    def pack(dest):
        def fill(i, _):
            packed[dest, i // 4, i // 2 % 2, pl.ds(i % 2 * 64, 64)] = crop[source[dest * 16 + i]]
            return 0

        lax.fori_loop(0, 16, fill, 0)

    across = [((x + 2) % 4) * 2 + (core + flip) % 2 for flip in range(2)]
    near = [
        (away, flip, ((x + away + 4) % 4) * 2 + (core + flip) % 2)
        for away in (1, -1)
        for flip in range(2)
    ]

    def cross_send(group):
        return [
            copies.start(
                packed.at[across[flip], group], cross.at[flip, group], at(y, z, x + turn, core)
            )
            for flip in range(2)
        ]

    def cross_pass(arriving, group):
        origin = ((x - turn + 4) % 4) * 2 + core
        passed = []
        for flip in range(2):
            arriving[flip].wait_recv()
            passed.append(
                copies.start(
                    cross.at[flip, group],
                    crops.at[group, :, origin],
                    at(y, z, x + turn, (core + flip) % 2),
                )
            )
        return passed

    def near_send(group):
        return [
            copies.start(
                packed.at[dest, group],
                crops.at[group, :, mine],
                at(y, z, x + away, (core + flip) % 2),
            )
            for away, flip, dest in near
        ] + [
            copies.start(
                packed.at[x * 2 + 1 - core, group],
                crops.at[group, :, mine],
                at(y, z, x, 1 - core),
            )
        ]

    crossing, crossed, nearby = {}, {}, {}
    for dest in across:
        pack(dest)
    crossing[0] = cross_send(0)
    for _, _, dest in near:
        pack(dest)
    pack(x * 2 + 1 - core)
    nearby[0] = near_send(0)
    crossing[1] = cross_send(1)
    halo.first()
    halo.own_rows()
    got = []
    for away in (1, 2, 3):
        for flip in range(2):
            to = (core + flip) % 2
            got.append(
                copies.start(
                    cells.at[((x + away) % 4) * 2 + to], places.at[mine], at(y, z, x + away, to)
                )
            )
    got.append(
        copies.start(cells.at[x * 2 + 1 - core], places.at[mine], at(y, z, x, 1 - core))
    )
    rest = [copies.start(shard, taps.at[lane(0)], at(y, z, x, 1 - core))]
    places[mine] = cells[mine]

    def keep(i, _):
        crops[i // 4, i // 2 % 2, mine, pl.ds(i % 2 * 64, 64)] = crop[source[mine * 16 + i]]
        return 0

    lax.fori_loop(0, 16, keep, 0)

    swaps = {}

    def swap(offset, y_to):
        piece = taps.at[lane(offset), :, half]
        swaps[offset] = copies.start(piece, piece, at(y_to, z, x, core))

    def ring_step(step):
        for way in (1, -1):
            ring[way].wait_recv()
            offset = -way * step
            if step < 3:
                piece = taps.at[lane(offset), :, half]
                ring[way] = copies.start(piece, piece, at(y, z + way, x, core))
            swap(offset, y + way)

    def whole(offset):
        swaps[offset].wait_recv()
        shard_all = taps.at[lane(offset)]
        rest.append(copies.start(shard_all, shard_all, at(y, z, x, 1 - core)))

    cell = lax.broadcasted_iota(jnp.int32, (512, 128), 0)

    def settle(group):
        for copy in nearby[group] + crossed[group] + (got if group == 0 else []):
            copy.wait_recv()
        for i in range(2):
            goal = 7 - group if i == 0 else group
            part[goal] = jnp.zeros_like(part[goal])

            def add(pair, _):
                hits = [
                    jnp.where(cell == places[2 * pair + j, 2 * group + i][None, :], 1.0, 0.0).astype(
                        jnp.bfloat16
                    )
                    for j in range(2)
                ]
                part[goal] += jnp.dot(
                    jnp.concatenate(hits, 1),
                    crops[group, i, pl.ds(2 * pair, 2)].reshape(256, 256),
                    preferred_element_type=jnp.float32,
                )
                return 0

            lax.fori_loop(0, 4, add, 0)

    def chain(goal, chunk, way):
        landing, leaving, sends, recvs = (
            (in_up, out_up, up_send, up_recv) if way == 1 else (in_down, out_down, down_send, down_recv)
        )
        return pltpu.make_async_remote_copy(
            src_ref=leaving.at[goal, chunk],
            dst_ref=landing.at[goal, chunk],
            send_sem=sends.at[goal, chunk],
            recv_sem=recvs.at[goal, chunk],
            device_id=at(y, z + way, x, core),
            device_id_type=MESH,
        )

    def turn_of(step, way):
        rank = strip if way == 1 else 7 - strip
        turn_at = step - rank + 16
        late = (turn_at - 16 + 32) % 32
        odd = late % 2
        ahead = (1 - odd) * (7 - late // 2) + odd * (late // 2)
        busy = (late < 8) & (late != 1) & (rank < ahead)
        return rank, (ahead if way == 1 else 7 - ahead), busy

    def advance(step, chunk, way):
        rank, goal, busy = turn_of(step, way)
        landing, leaving = (in_up, out_up) if way == 1 else (in_down, out_down)

        @pl.when(busy)
        def _():
            copy = chain(goal, chunk, way)
            mid = part[goal, pl.ds(chunk * 256, 256)]

            @pl.when(rank > 0)
            def _():
                copy.wait_recv()
                leaving[goal, chunk] = (mid + landing[goal, chunk].astype(jnp.float32)).astype(
                    jnp.bfloat16
                )

            @pl.when(rank == 0)
            def _():
                leaving[goal, chunk] = mid.astype(jnp.bfloat16)

            copy.start()

    def slot(step):
        for chunk in range(2):
            for way in (1, -1):
                advance(step, chunk, way)

    ring_step(1)
    crossed[0] = cross_pass(crossing[0], 0)
    nearby[1] = near_send(1)
    crossing[2] = cross_send(2)
    ring_step(2)
    settle(0)
    slot(0)
    ring_step(3)
    far = taps.at[lane(4), :, half]
    piece = taps.at[lane(-3 * turn), :, half]
    ring_last = copies.start(piece, piece, at(y, z + turn, x, core))
    crossed[1] = cross_pass(crossing[1], 1)
    nearby[2] = near_send(2)
    crossing[3] = cross_send(3)
    halo.forward()
    slot(1)
    ring_last.wait_recv()
    swaps[4] = copies.start(far, far, at(y + turn, z, x, core))
    for offset in (1, -1, 2, -2):
        whole(offset)
    settle(1)
    slot(2)
    crossed[2] = cross_pass(crossing[2], 2)
    nearby[3] = near_send(3)
    slot(3)
    for offset in (3, -3, 4):
        whole(offset)
    settle(2)
    slot(4)
    crossed[3] = cross_pass(crossing[3], 3)
    slot(5)
    settle(3)
    slot(6)
    halo.near_columns()
    slot(7)
    halo.far_rows()
    slot(8)
    halo.finish()
    slot(9)
    assert copies.used == SENDS, copies.used
    for chunk in range(2):
        total[chunk] = part[strip, pl.ds(chunk * 256, 256)]
        for way in (1, -1):
            landing = in_up if way == 1 else in_down

            @pl.when((strip if way == 1 else 7 - strip) > 0)
            def _():
                chain(strip, chunk, way).wait_recv()
                total[chunk] += landing[strip, chunk].astype(jnp.float32)

    for copy in rest:
        copy.wait_recv()
    own_shard.wait()
    for step in range(10):
        for chunk in range(2):
            for way in (1, -1):
                rank, goal, busy = turn_of(step, way)

                @pl.when(busy)
                def _():
                    chain(goal, chunk, way).wait_send()

    for copy in copies.sent:
        copy.wait_send()


SENDS = 75


def return_kernel(tile, ext, left, right, relay, edge, send_sems, recv_sems):
    copies = Copies(send_sems, recv_sems)
    greet(halo_partners())
    halo = Halo(copies, tile, ext, left, right, relay, edge, 0, 2, -1)
    halo.first()
    halo.own_rows()
    halo.forward()
    halo.near_columns()
    halo.far_rows()
    halo.finish()
    for copy in copies.sent:
        copy.wait_send()


def ones_where(hit):
    return jnp.where(hit, 1.0, 0.0).astype(jnp.bfloat16)


def exact(pick, rows):
    return jnp.dot(pick, rows, preferred_element_type=jnp.float32)


def widen(ext, left, right, wide, far, far_there):
    _, _, x, _ = place()
    strip = lax.axis_index("wa")
    cell = lax.broadcasted_iota(jnp.int32, (288, 288), 0)
    other = lax.broadcasted_iota(jnp.int32, (288, 288), 1)
    back = ones_where((other == cell - 1) & (cell % 16 != 0))
    ahead = ones_where((other == cell + 1) & (cell % 16 != 15))
    cell = lax.broadcasted_iota(jnp.int32, (288, 32), 0)
    other = lax.broadcasted_iota(jnp.int32, (288, 32), 1)
    from_left = ones_where(cell == other * 16 + jnp.where(strip > 0, 0, 4096))
    from_right = ones_where(cell == other * 16 + 15 + jnp.where(strip < 15, 0, 4096))
    row = lax.broadcasted_iota(jnp.int32, (288, 256), 0) // 16
    low, high = jnp.where(x > 0, 0, 1), jnp.where(x < 3, 17, 16)
    for frame in range(4):
        least = jnp.where(far_there, low, 99) if frame in far else low
        there = (row >= least) & (row <= high)
        flat = ext[frame].reshape(288, 256)
        parts = (
            exact(back, flat) + exact(from_left, left[frame]),
            flat.astype(jnp.float32),
            exact(ahead, flat) + exact(from_right, right[frame]),
        )
        for shift, value in enumerate(parts):
            wide[frame, :, :, 256 * shift : 256 * shift + 256] = (
                jnp.where(there, value, 0.0).astype(jnp.bfloat16).reshape(18, 16, 256)
            )


NT = (((1,), (1,)), ((), ()))


def forward_kernel(ext, left, right, taps, down, grad_out, reduced, grad_pre, spread, wide):
    widen(ext, left, right, wide, (0, 1), lax.axis_index("ta") > 0)
    preact = jnp.zeros((512, 256), jnp.float32)
    for a in range(3):
        for b in range(3):
            preact += jnp.dot(
                wide[a : a + 2, b : b + 16].reshape(512, 768),
                taps[a * 3 + b],
                preferred_element_type=jnp.float32,
            )
    sig = jax.nn.sigmoid(preact)
    own = ext[2:4, 1:17].reshape(512, 256).astype(jnp.float32)
    section = (own + preact * sig).astype(jnp.bfloat16)
    small = lax.broadcasted_iota(jnp.int32, (128, 512), 0)
    large = lax.broadcasted_iota(jnp.int32, (128, 512), 1)
    first = small // 64 * 256 + small // 8 % 8 * 32 + small % 8 * 2
    pooled = [
        exact(ones_where(large == first + p * 16 + q), section).astype(jnp.bfloat16)
        for p in range(2)
        for q in range(2)
    ]
    reduced[...] = jnp.dot(
        jnp.concatenate(pooled, 1), down[...].reshape(1024, 256), preferred_element_type=jnp.float32
    ).astype(jnp.bfloat16)
    large = lax.broadcasted_iota(jnp.int32, (512, 128), 0)
    small = lax.broadcasted_iota(jnp.int32, (512, 128), 1)
    over = ones_where(small == large // 256 * 64 + large // 32 % 8 * 8 + large // 2 % 8)
    repeated = exact(over, grad_out[...]).astype(jnp.bfloat16)
    cell = lax.broadcasted_iota(jnp.int32, (512, 256), 0)
    kind = cell // 16 % 2 * 2 + cell % 2
    back = jnp.zeros((512, 256), jnp.float32)
    for which in range(4):
        back = jnp.where(
            kind == which,
            lax.dot_general(repeated, down[which], NT, preferred_element_type=jnp.float32),
            back,
        )
    spread[...] = back
    grad_pre[...] = (back * sig * (1.0 + preact * (1.0 - sig))).astype(jnp.bfloat16)


def backward_kernel(ext, left, right, taps, spread, total, grad_in, wide):
    widen(ext, left, right, wide, (2, 3), lax.axis_index("ta") < 7)
    summed = spread[...] + total[...].reshape(512, 256)
    for a in range(3):
        for b in range(3):
            for c in range(3):
                summed += lax.dot_general(
                    wide[2 - a : 4 - a, 2 - b : 18 - b, :, 256 * (2 - c) : 256 * (3 - c)].reshape(
                        512, 256
                    ),
                    taps[(a * 3 + b) * 3 + c],
                    NT,
                    preferred_element_type=jnp.float32,
                )
    grad_in[...] = summed.astype(jnp.bfloat16)


VM = functools.partial(pl.BlockSpec, memory_space=pltpu.VMEM)
SM = functools.partial(pl.BlockSpec, memory_space=pltpu.SMEM)
ANY = functools.partial(pl.BlockSpec, memory_space=pl.ANY)
DMA = pltpu.SemaphoreType.DMA


def per_device(
    features, conv_weight, down_weight, grad_out, crop_grad,
    crop_owner, crop_frame, crop_row, crop_col, crop_valid,
):
    frames, rows, cols, width = features.shape
    half_type, shape = jnp.bfloat16, jax.ShapeDtypeStruct
    source, cells = pl.pallas_call(
        table_kernel,
        out_shape=(shape((128,), jnp.int32), shape((64, 128), jnp.int32)),
        in_specs=[ANY()] * 5,
        out_specs=(SM(), VM()),
        scratch_shapes=[
            pltpu.SMEM((5, 64), jnp.int32),
            pltpu.SMEM((64,), jnp.int32),
            pltpu.SMEM((128,), jnp.int32),
            DMA((5,)),
        ],
    )(crop_owner[:, 0], crop_frame, crop_row, crop_col, crop_valid)
    ext_shape = shape((4, rows + 2, cols, width), half_type)
    side_shape = shape((4, 32, width), half_type)
    relay = pltpu.VMEM((2, rows, cols, width), half_type)
    edge = pltpu.VMEM((2, 4, 32, width), half_type)
    chain = pltpu.VMEM((8, 2, 256, width), half_type)
    ext, left, right, taps, total = pl.pallas_call(
        gather_kernel,
        out_shape=(
            ext_shape, side_shape, side_shape,
            shape((16, 432, width), half_type),
            shape((2, 256, width), jnp.float32),
        ),
        in_specs=[VM(), VM(), SM(), VM(), ANY()],
        out_specs=(VM(), VM(), VM(), ANY(), VM()),
        scratch_shapes=[
            relay, edge,
            pltpu.VMEM((65, 64, width), half_type),
            pltpu.VMEM((8, 4, 2, 128, width), half_type),
            pltpu.VMEM((4, 2, 8, 128, width), half_type),
            pltpu.VMEM((8, 8, 128), jnp.int32),
            pltpu.VMEM((2, 4, 2, 128, width), half_type),
            pltpu.VMEM((8, 512, width), jnp.float32),
            chain, chain, chain, chain,
            DMA((SENDS,)), DMA((SENDS,)), DMA((2,)),
            DMA((8, 2)), DMA((8, 2)), DMA((8, 2)), DMA((8, 2)),
        ],
        compiler_params=pltpu.CompilerParams(
            collective_id=0, has_side_effects=True, vmem_limit_bytes=40 << 20
        ),
    )(features, conv_weight, source, cells.reshape(8, 8, 128), crop_grad.reshape(64, 64, width))
    wide = pltpu.VMEM((4, rows + 2, cols, 3 * width), half_type)
    roomy = pltpu.CompilerParams(vmem_limit_bytes=32 << 20)
    cells_all = frames * rows * cols
    reduced, grad_pre, spread = pl.pallas_call(
        forward_kernel,
        out_shape=(
            shape((cells_all // 4, width), half_type),
            shape((cells_all, width), half_type),
            shape((cells_all, width), jnp.float32),
        ),
        in_specs=[VM()] * 6,
        out_specs=(VM(), VM(), VM()),
        scratch_shapes=[wide],
        compiler_params=roomy,
    )(
        ext, left, right, taps.reshape(9, 3 * width, width),
        down_weight.reshape(4, width, width), grad_out.reshape(-1, width),
    )
    ext, left, right = pl.pallas_call(
        return_kernel,
        out_shape=(ext_shape, side_shape, side_shape),
        in_specs=[VM()],
        out_specs=(VM(), VM(), VM()),
        scratch_shapes=[relay, edge, DMA((10,)), DMA((10,))],
        compiler_params=pltpu.CompilerParams(
            collective_id=1, has_side_effects=True, vmem_limit_bytes=32 << 20
        ),
    )(grad_pre.reshape(frames, rows, cols, width))
    grad_in = pl.pallas_call(
        backward_kernel,
        out_shape=shape((cells_all, width), half_type),
        in_specs=[VM()] * 6,
        out_specs=VM(),
        scratch_shapes=[wide],
        compiler_params=roomy,
    )(ext, left, right, taps.reshape(27, width, width), spread, total)
    return (
        reduced.reshape(frames, rows // 2, cols // 2, width),
        grad_in.reshape(frames, rows, cols, width),
    )


def solution(mesh):
    spread_all = ("ta", "ha", "wa")
    tile = P("ta", "ha", "wa", None)
    in_specs = (
        tile, P("wa", None), P(), tile, P(spread_all, None, None, None), P(spread_all, None),
        P(spread_all), P(spread_all), P(spread_all), P(spread_all),
    )
    return jax.shard_map(
        per_device, mesh=mesh, in_specs=in_specs, out_specs=(tile, tile), check_vma=False
    )
```

```python
import jax
import jax.numpy as jnp
from jax import lax
from jax.experimental import pallas as pl
from jax.experimental.pallas import tpu as pltpu
from jax.sharding import PartitionSpec as P

MESH = pl.DeviceIdType.MESH
CAP = 2


def place():
    slab, x, strip = lax.axis_index("ta"), lax.axis_index("ha"), lax.axis_index("wa")
    return slab // 2, (slab % 2) * 8 + strip // 2, x, strip % 2


def at(y, z, x, core):
    y, z, x = (y + 4) % 4, (z + 16) % 16, (x + 4) % 4
    return (y * 2 + z // 8, x, (z % 8) * 2 + core)


class Copies:
    def __init__(self, send_sems, recv_sems):
        self.send_sems, self.recv_sems, self.used, self.sent = send_sems, recv_sems, 0, []

    def make(self, src, dst, device):
        slot = self.used
        self.used += 1
        return pltpu.make_async_remote_copy(
            src_ref=src,
            dst_ref=dst,
            send_sem=self.send_sems.at[slot],
            recv_sem=self.recv_sems.at[slot],
            device_id=device,
            device_id_type=MESH,
        )

    def start(self, src, dst, device):
        copy = self.make(src, dst, device)
        copy.start()
        self.sent.append(copy)
        return copy


def greet(devices):
    barrier = pltpu.get_barrier_semaphore()
    for device in devices:
        pl.semaphore_signal(barrier, inc=1, device_id=device, device_id_type=MESH)
    return lambda: pl.semaphore_wait(barrier, len(devices))


def edge_columns(ext, edge, frame):
    rows, cols, width = ext.shape[1:]
    flat = ext[frame].reshape(rows * cols, width)
    row = lax.broadcasted_iota(jnp.int32, (edge.shape[2], rows * cols), 0)
    cell = lax.broadcasted_iota(jnp.int32, (edge.shape[2], rows * cols), 1)
    for side, col in ((0, 0), (1, cols - 1)):
        pick = jnp.where(cell == row * cols + col, 1.0, 0.0).astype(jnp.bfloat16)
        edge[side, frame] = jnp.dot(pick, flat, preferred_element_type=jnp.float32).astype(
            jnp.bfloat16
        )


FAR = ((0, 1), (15, 1), (1, 5), (6, 5), (11, 4))


class Halo:
    def __init__(self, copies, tile, ext, left, right, edge, own, step):
        self.copies, self.tile, self.ext, self.left, self.right = copies, tile, ext, left, right
        self.edge, self.own, self.other, self.step = edge, own, 2 - own, step
        self.far = []

    def send_far(self, piece):
        y, z, x, core = place()
        y_to = y + z // 8 if self.step == 1 else y - 1 + z // 8
        first, count = FAR[piece]
        for frame in range(2):
            self.far.append(
                self.copies.start(
                    self.tile.at[frame, pl.ds(first, count)],
                    self.ext.at[self.other + frame, pl.ds(1 + first, count)],
                    at(y_to, z + 8, x, core),
                )
            )

    def own_rows(self):
        y, z, x, core = place()
        ext, own = self.ext, self.own
        self.rows_own = [
            self.copies.start(
                self.tile.at[:, pl.ds(15, 1)],
                ext.at[pl.ds(own, 2), pl.ds(0, 1)],
                at(y, z, x + 1, core),
            ),
            self.copies.start(
                self.tile.at[:, pl.ds(0, 1)],
                ext.at[pl.ds(own, 2), pl.ds(17, 1)],
                at(y, z, x - 1, core),
            ),
        ]

    def sides(self, first):
        y, z, x, core = place()
        two = pl.ds(first, 2)
        return [
            self.copies.start(
                self.edge.at[1, two], self.left.at[two], at(y, z + core, x, 1 - core)
            ),
            self.copies.start(
                self.edge.at[0, two], self.right.at[two], at(y, z - 1 + core, x, 1 - core)
            ),
        ]

    def near_columns(self):
        for copy in self.rows_own:
            copy.wait_recv()
        for frame in range(2):
            edge_columns(self.ext, self.edge, self.own + frame)
        self.near_sides = self.sides(self.own)

    def far_rows(self):
        y, z, x, core = place()
        ext, two = self.ext, pl.ds(self.other, 2)
        for copy in self.far[:4]:
            copy.wait_recv()
        self.borders = [
            self.copies.start(
                ext.at[two, pl.ds(16, 1)], ext.at[two, pl.ds(0, 1)], at(y, z, x + 1, core)
            ),
            self.copies.start(
                ext.at[two, pl.ds(1, 1)], ext.at[two, pl.ds(17, 1)], at(y, z, x - 1, core)
            ),
        ]

    def far_columns(self):
        for copy in self.far[4:] + self.borders:
            copy.wait_recv()
        for frame in range(2):
            edge_columns(self.ext, self.edge, self.other + frame)
        self.far_sides = self.sides(self.other)


def partners():
    y, z, x, core = place()
    return [
        at(y, z + 8, x, core),
        at(y + 1, z + 8, x, core),
        at(y - 1, z + 8, x, core),
        at(y, z, x + 1, core),
        at(y, z, x - 1, core),
        at(y, z, x + 1, 1 - core),
        at(y, z, x - 1, 1 - core),
        at(y, z, x + 2, core),
        at(y, z, x + 2, 1 - core),
        at(y, z, x, 1 - core),
        at(y, z + 1, x, core),
        at(y, z - 1, x, core),
        at(y, z - 1 + 2 * core, x, 1 - core),
        at(y + 1, z, x, core),
        at(y - 1, z, x, core),
    ]


def iota(shape, axis):
    return lax.broadcasted_iota(jnp.int32, shape, axis)


def ones_where(hit):
    return jnp.where(hit, 1.0, 0.0).astype(jnp.bfloat16)


def exact(pick, rows):
    return jnp.dot(pick, rows, preferred_element_type=jnp.float32)


def lay_out(index, source, cells):
    owner, frame, row, col, valid = [index[pl.ds(i, 1), pl.ds(0, 64)] for i in range(5)]
    one, other = iota((64, 64), 0), iota((64, 64), 1)

    def column(line):
        return jnp.sum(jnp.where(one == other, line, 0), 1, keepdims=True)

    before = (column(owner) == owner) & (one < other) & (column(valid) != 0)
    rank = jnp.sum(jnp.where(before, 1, 0), 0, keepdims=True)
    deep = (owner & 15) >> 1
    spot = jnp.where(deep < 4, 2 * deep + 1, 2 * (7 - deep))
    slot = (((owner >> 4) * 2 + (owner & 1)) * 8 + spot) * 2 + rank
    slot = jnp.where(valid != 0, slot, 999)
    hit = column(slot) == iota((64, 128), 1)
    source[...] = 64 + jnp.sum(jnp.where(hit, iota((64, 128), 0) - 64, 0), 0, keepdims=True)
    base = frame * 256 + row * 16 + col
    bases = [
        jnp.sum(jnp.where(slot == one * 2 + i, base, 0), 1, keepdims=True) for i in range(2)
    ]
    where = iota((64, 128), 1)
    offset = (where & 63) // 8 * 16 + (where & 7)
    cells[...] = (offset + jnp.where(where < 64, bases[0], bases[1])).reshape(8, 8, 128)


def widen(halo, wide, frames, far_there):
    _, _, x, _ = place()
    strip = lax.axis_index("wa")
    cell, other = iota((288, 288), 0), iota((288, 288), 1)
    back = ones_where((other == cell - 1) & (cell % 16 != 0))
    ahead = ones_where((other == cell + 1) & (cell % 16 != 15))
    cell, other = iota((288, 32), 0), iota((288, 32), 1)
    from_left = ones_where(cell == other * 16 + jnp.where(strip > 0, 0, 4096))
    from_right = ones_where(cell == other * 16 + 15 + jnp.where(strip < 15, 0, 4096))
    row = iota((288, 256), 0) // 16
    low, high = jnp.where(x > 0, 0, 1), jnp.where(x < 3, 17, 16)
    for frame in frames:
        far = halo.other <= frame < halo.other + 2
        least = jnp.where(far_there, low, 99) if far else low
        there = (row >= least) & (row <= high)
        flat = halo.ext[frame].reshape(288, 256)
        parts = (
            exact(back, flat) + exact(from_left, halo.left[frame]),
            flat.astype(jnp.float32),
            exact(ahead, flat) + exact(from_right, halo.right[frame]),
        )
        for shift, value in enumerate(parts):
            wide[frame, :, :, 256 * shift : 256 * shift + 256] = (
                jnp.where(there, value, 0.0).astype(jnp.bfloat16).reshape(18, 16, 256)
            )


NT = (((1,), (1,)), ((), ()))


def conv_part(wide, taps, acc, a, first, count, out):
    summed = jnp.zeros((count * 256, 256), jnp.float32)
    for b in range(3):
        at_row = (a * 3 + b) * 768
        summed += jnp.dot(
            wide[first : first + count, b : b + 16].reshape(count * 256, 768),
            taps[at_row : at_row + 768],
            preferred_element_type=jnp.float32,
        )
    acc[out * 256 : (out + count) * 256] += summed


def back_part(wide, taps, acc, a, first, count, out):
    summed = jnp.zeros((count * 256, 256), jnp.float32)
    for b in range(3):
        for c in range(3):
            at_row = ((a * 3 + b) * 3 + c) * 256
            lanes = slice(256 * (2 - c), 256 * (3 - c))
            summed += lax.dot_general(
                wide[first : first + count, 2 - b : 18 - b, :, lanes].reshape(count * 256, 256),
                taps[at_row : at_row + 256],
                NT,
                preferred_element_type=jnp.float32,
            )
    acc[out * 256 : (out + count) * 256] += summed


def middle(preact, tile, down, reduced, grad_pre, acc):
    sig = jax.nn.sigmoid(preact)
    section = (tile[...].reshape(512, 256).astype(jnp.float32) + preact * sig).astype(jnp.bfloat16)
    small, large = iota((128, 512), 0), iota((128, 512), 1)
    first = small // 64 * 256 + small // 8 % 8 * 32 + small % 8 * 2
    pooled = [
        exact(ones_where(large == first + p * 16 + q), section).astype(jnp.bfloat16)
        for p in range(2)
        for q in range(2)
    ]
    reduced[...] = jnp.dot(
        jnp.concatenate(pooled, 1), down[...].reshape(1024, 256), preferred_element_type=jnp.float32
    ).astype(jnp.bfloat16)
    spread = acc[...]
    grad_pre[...] = (spread * sig * (1.0 + preact * (1.0 - sig))).astype(jnp.bfloat16).reshape(
        2, 16, 16, 256
    )


def spread_out(down, grad_out, acc):
    large, small = iota((512, 128), 0), iota((512, 128), 1)
    over = ones_where(small == large // 256 * 64 + large // 32 % 8 * 8 + large // 2 % 8)
    repeated = exact(over, grad_out[...]).astype(jnp.bfloat16)
    cell = iota((512, 256), 0)
    kind = cell // 16 % 2 * 2 + cell % 2
    back = jnp.zeros((512, 256), jnp.float32)
    for which in range(4):
        back = jnp.where(
            kind == which,
            lax.dot_general(repeated, down[which], NT, preferred_element_type=jnp.float32),
            back,
        )
    acc[...] = back


def step_kernel(
    features, weight, indices, crop_grad, down_all, grad_all, reduced, grad_in,
    tile, index, down, grad_out, table, source, cells,
    ext, left, right, edge, ext_b, left_b, right_b, edge_b, grad_pre,
    wide, taps, preact, acc, crop, packed, crops, places, part,
    in_up, in_down, out_up, out_down,
    send_sems, recv_sems, local_sems, up_send, up_recv, down_send, down_recv,
):
    y, z, x, core = place()
    strip = z % 8
    mine = x * 2 + core
    slab = lax.axis_index("ta")
    copies = Copies(send_sems, recv_sems)

    def lane(offset):
        return pl.ds(pl.multiple_of((((strip + offset + 8) % 8) * 2 + core) * 432, 16), 432)

    loads = [
        pltpu.make_async_copy(src, dst, local_sems.at[i])
        for i, (src, dst) in enumerate(
            (
                (indices, index),
                (crop_grad, crop.at[pl.ds(0, 64)]),
                (features, tile),
                (weight, taps.at[lane(0)]),
                (down_all, down),
                (grad_all, grad_out),
            )
        )
    ]
    for load in loads:
        load.start()
    met = greet(partners())
    crop[64] = jnp.zeros_like(crop[64])
    loads[0].wait()
    lay_out(index, table, cells)
    to_scalars = pltpu.make_async_copy(table, source, local_sems.at[6])
    to_scalars.start()
    places[mine] = cells[mine]
    loads[2].wait()
    ext[2:4, 1:17] = tile[...]
    loads[1].wait()
    to_scalars.wait()

    near = [
        (away, flip, ((x + away + 4) % 4) * 2 + (core + flip) % 2)
        for away in (2, 1, -1)
        for flip in range(2)
    ] + [(0, 1, x * 2 + 1 - core)]

    def pack(dest):
        def fill(i, _):
            packed[dest, i // 4, i // 2 % 2, pl.ds(i % 2 * 64, 64)] = crop[source[0, dest * 16 + i]]
            return 0

        lax.fori_loop(0, 16, fill, 0)

    for _, _, dest in near:
        pack(dest)

    def keep(i, _):
        crops[i // 4, i // 2 % 2, mine, pl.ds(i % 2 * 64, 64)] = crop[source[0, mine * 16 + i]]
        return 0

    lax.fori_loop(0, 16, keep, 0)
    for load in loads[3:]:
        load.wait()
    halo = Halo(copies, tile, ext, left, right, edge, 2, 1)
    back = Halo(copies, grad_pre, ext_b, left_b, right_b, edge_b, 0, -1)
    half = pl.ds(pl.multiple_of((y % 2) * 128, 128), 128)
    turn = 1 - 2 * core

    def crops_send(group):
        return [
            copies.start(
                packed.at[dest, group],
                crops.at[group, :, mine],
                at(y, z, x + away, (core + flip) % 2),
            )
            for away, flip, dest in near
        ]

    met()
    arriving, ring, swaps = {}, {}, {}
    halo.send_far(0)
    halo.send_far(1)
    for way in (1, -1):
        piece = taps.at[lane(0), half]
        ring[way] = copies.start(piece, piece, at(y, z + way, x, core))
    halo.own_rows()
    marks = [
        copies.start(cells.at[dest], places.at[mine], at(y, z, x + away, (core + flip) % 2))
        for away, flip, dest in near
    ]
    arriving[0] = crops_send(0)
    halo.send_far(2)
    rest = [copies.start(taps.at[lane(0)], taps.at[lane(0)], at(y, z, x, 1 - core))]

    def swap(offset, y_to):
        piece = taps.at[lane(offset), half]
        swaps[offset] = copies.start(piece, piece, at(y_to, z, x, core))

    def ring_step(step):
        for way in (1, -1):
            ring[way].wait_recv()
            offset = -way * step
            if step < 3:
                piece = taps.at[lane(offset), half]
                ring[way] = copies.start(piece, piece, at(y, z + way, x, core))
            swap(offset, y + way)

    def whole(offset):
        swaps[offset].wait_recv()
        shard_all = taps.at[lane(offset)]
        rest.append(copies.start(shard_all, shard_all, at(y, z, x, 1 - core)))

    cell = iota((512, 128), 0)

    def settle(group):
        for copy in arriving[group] + (marks if group == 0 else []):
            copy.wait_recv()
        for i in range(2):
            goal = 7 - group if i == 0 else group
            part[goal] = jnp.zeros_like(part[goal])

            def add(pair, _):
                hits = [
                    ones_where(cell == places[2 * pair + j, 2 * group + i][None, :])
                    for j in range(2)
                ]
                part[goal] += jnp.dot(
                    jnp.concatenate(hits, 1),
                    crops[group, i, pl.ds(2 * pair, 2)].reshape(256, 256),
                    preferred_element_type=jnp.float32,
                )
                return 0

            lax.fori_loop(0, 4, add, 0)

    def chain(goal, chunk, way):
        landing, leaving, sends, recvs = (
            (in_up, out_up, up_send, up_recv) if way == 1 else (in_down, out_down, down_send, down_recv)
        )
        return pltpu.make_async_remote_copy(
            src_ref=leaving.at[goal, chunk],
            dst_ref=landing.at[goal, chunk],
            send_sem=sends.at[goal, chunk],
            recv_sem=recvs.at[goal, chunk],
            device_id=at(y, z + way, x, core),
            device_id_type=MESH,
        )

    def turn_of(step, way):
        rank = strip if way == 1 else 7 - strip
        turn_at = step - rank + 16
        late = (turn_at - 16 + 32) % 32
        odd = late % 2
        ahead = (1 - odd) * (7 - late // 2) + odd * (late // 2)
        busy = (late < 8) & (late != 1) & (rank < ahead)
        return rank, (ahead if way == 1 else 7 - ahead), busy

    def advance(step, chunk, way):
        rank, goal, busy = turn_of(step, way)
        landing, leaving = (in_up, out_up) if way == 1 else (in_down, out_down)

        @pl.when(busy)
        def _():
            copy = chain(goal, chunk, way)
            mid = part[goal, pl.ds(chunk * 256, 256)]

            @pl.when(rank > 0)
            def _():
                copy.wait_recv()
                leaving[goal, chunk] = (mid + landing[goal, chunk].astype(jnp.float32)).astype(
                    jnp.bfloat16
                )

            @pl.when(rank == 0)
            def _():
                leaving[goal, chunk] = mid.astype(jnp.bfloat16)

            copy.start()

    def slot(step):
        for chunk in range(2):
            for way in (1, -1):
                advance(step, chunk, way)

    ring_step(1)
    halo.send_far(3)
    halo.far_rows()
    arriving[1] = crops_send(1)
    halo.near_columns()
    ring_step(2)
    halo.send_far(4)
    spread_out(down, grad_out, acc)
    settle(0)
    slot(0)
    arriving[2] = crops_send(2)
    ring_step(3)
    piece = taps.at[lane(-3 * turn), half]
    ring_last = copies.start(piece, piece, at(y, z + turn, x, core))
    for offset in (1, -1, 2, -2):
        whole(offset)
    slot(1)
    ring_last.wait_recv()
    swap(4, y + turn)
    settle(1)
    slot(2)
    arriving[3] = crops_send(3)
    for offset in (3, -3, 4):
        whole(offset)
    for copy in halo.near_sides + rest:
        copy.wait_recv()
    preact[...] = jnp.zeros_like(preact)
    widen(halo, wide, (2, 3), slab > 0)
    conv_part(wide, taps, preact, 2, 2, 2, 0)
    slot(3)
    conv_part(wide, taps, preact, 1, 2, 1, 1)
    halo.far_columns()
    settle(2)
    slot(4)
    for copy in halo.far_sides:
        copy.wait_recv()
    widen(halo, wide, (0, 1), slab > 0)
    conv_part(wide, taps, preact, 0, 0, 2, 0)
    conv_part(wide, taps, preact, 1, 1, 1, 0)
    middle(preact[...], tile, down, reduced, grad_pre, acc)
    back.send_far(0)
    back.send_far(1)
    back.own_rows()
    back.send_far(2)
    ext_b[0:2, 1:17] = grad_pre[...]
    slot(5)
    back.send_far(3)
    settle(3)
    slot(6)
    back.near_columns()
    back.send_far(4)
    slot(7)
    back.far_rows()
    slot(8)
    for copy in back.near_sides:
        copy.wait_recv()
    widen(back, wide, (0, 1), slab < 7)
    slot(9)
    back_part(wide, taps, acc, 2, 0, 2, 0)
    back_part(wide, taps, acc, 1, 1, 1, 0)
    back.far_columns()
    assert copies.used == SENDS, copies.used
    for chunk in range(2):
        place_at = pl.ds(chunk * 256, 256)
        acc[place_at] += part[strip, place_at]
        for way in (1, -1):
            landing = in_up if way == 1 else in_down

            @pl.when((strip if way == 1 else 7 - strip) > 0)
            def _():
                chain(strip, chunk, way).wait_recv()
                acc[place_at] += landing[strip, chunk].astype(jnp.float32)

    for copy in back.far_sides:
        copy.wait_recv()
    widen(back, wide, (2, 3), slab < 7)
    back_part(wide, taps, acc, 0, 2, 2, 0)
    back_part(wide, taps, acc, 1, 2, 1, 1)
    grad_in[...] = acc[...].astype(jnp.bfloat16)
    for step in range(10):
        for chunk in range(2):
            for way in (1, -1):
                rank, goal, busy = turn_of(step, way)

                @pl.when(busy)
                def _():
                    chain(goal, chunk, way).wait_send()

    for copy in copies.sent:
        copy.wait_send()


SENDS = 93
DMA = pltpu.SemaphoreType.DMA


def per_device(
    features, conv_weight, down_weight, grad_out, crop_grad,
    crop_owner, crop_frame, crop_row, crop_col, crop_valid,
):
    frames, rows, cols, width = features.shape
    half_type, shape, vmem = jnp.bfloat16, jax.ShapeDtypeStruct, pltpu.VMEM
    indices = jnp.stack(
        [crop_owner[:, 0], crop_frame, crop_row, crop_col, crop_valid] + [crop_valid] * 3, 0
    )
    indices = jnp.pad(indices, ((0, 0), (0, 64)))
    halo = [
        vmem((4, 18, 16, width), half_type), vmem((4, 32, width), half_type),
        vmem((4, 32, width), half_type), vmem((2, 4, 32, width), half_type),
    ]
    tile = vmem((2, 16, 16, width), half_type)
    chain = vmem((8, 2, 256, width), half_type)
    reduced, grad_in = pl.pallas_call(
        step_kernel,
        out_shape=(shape((128, width), half_type), shape((512, width), half_type)),
        in_specs=[pl.BlockSpec(memory_space=pl.ANY)] * 6,
        out_specs=[pl.BlockSpec(memory_space=pltpu.VMEM)] * 2,
        scratch_shapes=[
            tile, vmem((8, 128), jnp.int32), vmem((4, width, width), half_type),
            vmem((128, width), half_type), vmem((1, 128), jnp.int32),
            pltpu.SMEM((1, 128), jnp.int32), vmem((8, 8, 128), jnp.int32),
            *halo, *halo, tile,
            vmem((4, 18, 16, 3 * width), half_type), vmem((6912, width), half_type),
            vmem((512, width), jnp.float32), vmem((512, width), jnp.float32),
            vmem((65, 64, width), half_type), vmem((8, 4, 2, 128, width), half_type),
            vmem((4, 2, 8, 128, width), half_type), vmem((8, 8, 128), jnp.int32),
            vmem((8, 512, width), jnp.float32),
            chain, chain, chain, chain,
            DMA((SENDS,)), DMA((SENDS,)), DMA((7,)),
            DMA((8, 2)), DMA((8, 2)), DMA((8, 2)), DMA((8, 2)),
        ],
        compiler_params=pltpu.CompilerParams(
            collective_id=0, has_side_effects=True, vmem_limit_bytes=60 << 20
        ),
    )(
        features, conv_weight, indices, crop_grad.reshape(64, 64, width),
        down_weight.reshape(4, width, width), grad_out.reshape(-1, width),
    )
    return (
        reduced.reshape(frames, rows // 2, cols // 2, width),
        grad_in.reshape(frames, rows, cols, width),
    )


def solution(mesh):
    spread_all = ("ta", "ha", "wa")
    tile = P("ta", "ha", "wa", None)
    in_specs = (
        tile, P("wa", None), P(), tile, P(spread_all, None, None, None), P(spread_all, None),
        P(spread_all), P(spread_all), P(spread_all), P(spread_all),
    )
    return jax.shard_map(
        per_device, mesh=mesh, in_specs=in_specs, out_specs=(tile, tile), check_vma=False
    )
```

```python
import jax
import jax.numpy as jnp
from jax import lax
from jax.experimental import pallas as pl
from jax.experimental.pallas import tpu as pltpu
from jax.sharding import PartitionSpec as P

MESH = pl.DeviceIdType.MESH
CAP = 2


def place():
    slab, x, strip = lax.axis_index("ta"), lax.axis_index("ha"), lax.axis_index("wa")
    return slab // 2, (slab % 2) * 8 + strip // 2, x, strip % 2


def at(y, z, x, core):
    y, z, x = (y + 4) % 4, (z + 16) % 16, (x + 4) % 4
    return (y * 2 + z // 8, x, (z % 8) * 2 + core)


class Copies:
    def __init__(self, send_sems, recv_sems):
        self.send_sems, self.recv_sems, self.used, self.sent = send_sems, recv_sems, 0, []

    def make(self, src, dst, device):
        slot = self.used
        self.used += 1
        return pltpu.make_async_remote_copy(
            src_ref=src,
            dst_ref=dst,
            send_sem=self.send_sems.at[slot],
            recv_sem=self.recv_sems.at[slot],
            device_id=device,
            device_id_type=MESH,
        )

    def start(self, src, dst, device):
        copy = self.make(src, dst, device)
        copy.start()
        self.sent.append(copy)
        return copy


def greet(devices):
    barrier = pltpu.get_barrier_semaphore()
    for device in devices:
        pl.semaphore_signal(barrier, inc=1, device_id=device, device_id_type=MESH)
    return lambda: pl.semaphore_wait(barrier, len(devices))


def edge_columns(ext, edge, frame):
    rows, cols, width = ext.shape[1:]
    flat = ext[frame].reshape(rows * cols, width)
    row = lax.broadcasted_iota(jnp.int32, (edge.shape[2], rows * cols), 0)
    cell = lax.broadcasted_iota(jnp.int32, (edge.shape[2], rows * cols), 1)
    for side, col in ((0, 0), (1, cols - 1)):
        pick = jnp.where(cell == row * cols + col, 1.0, 0.0).astype(jnp.bfloat16)
        edge[side, frame] = jnp.dot(pick, flat, preferred_element_type=jnp.float32).astype(
            jnp.bfloat16
        )


FAR = ((0, 1), (15, 1), (1, 5), (6, 5), (11, 4))


class Halo:
    def __init__(self, copies, tile, ext, left, right, edge, own, step):
        self.copies, self.tile, self.ext, self.left, self.right = copies, tile, ext, left, right
        self.edge, self.own, self.other, self.step = edge, own, 2 - own, step
        self.far = []

    def send_far(self, piece):
        y, z, x, core = place()
        y_to = y + z // 8 if self.step == 1 else y - 1 + z // 8
        first, count = FAR[piece]
        for frame in range(2):
            self.far.append(
                self.copies.start(
                    self.tile.at[frame, pl.ds(first, count)],
                    self.ext.at[self.other + frame, pl.ds(1 + first, count)],
                    at(y_to, z + 8, x, core),
                )
            )

    def own_rows(self):
        y, z, x, core = place()
        ext, own = self.ext, self.own
        self.rows_own = [
            self.copies.start(
                self.tile.at[:, pl.ds(15, 1)],
                ext.at[pl.ds(own, 2), pl.ds(0, 1)],
                at(y, z, x + 1, core),
            ),
            self.copies.start(
                self.tile.at[:, pl.ds(0, 1)],
                ext.at[pl.ds(own, 2), pl.ds(17, 1)],
                at(y, z, x - 1, core),
            ),
        ]

    def sides(self, first):
        y, z, x, core = place()
        two = pl.ds(first, 2)
        return [
            self.copies.start(
                self.edge.at[1, two], self.left.at[two], at(y, z + core, x, 1 - core)
            ),
            self.copies.start(
                self.edge.at[0, two], self.right.at[two], at(y, z - 1 + core, x, 1 - core)
            ),
        ]

    def near_columns(self):
        for copy in self.rows_own:
            copy.wait_recv()
        for frame in range(2):
            edge_columns(self.ext, self.edge, self.own + frame)
        self.near_sides = self.sides(self.own)

    def far_rows(self):
        y, z, x, core = place()
        ext, two = self.ext, pl.ds(self.other, 2)
        for copy in self.far[:4]:
            copy.wait_recv()
        self.borders = [
            self.copies.start(
                ext.at[two, pl.ds(16, 1)], ext.at[two, pl.ds(0, 1)], at(y, z, x + 1, core)
            ),
            self.copies.start(
                ext.at[two, pl.ds(1, 1)], ext.at[two, pl.ds(17, 1)], at(y, z, x - 1, core)
            ),
        ]

    def far_columns(self):
        for copy in self.far[4:] + self.borders:
            copy.wait_recv()
        for frame in range(2):
            edge_columns(self.ext, self.edge, self.other + frame)
        self.far_sides = self.sides(self.other)


def partners():
    y, z, x, core = place()
    return [
        at(y, z + 8, x, core),
        at(y + 1, z + 8, x, core),
        at(y - 1, z + 8, x, core),
        at(y, z, x + 1, core),
        at(y, z, x - 1, core),
        at(y, z, x + 1, 1 - core),
        at(y, z, x - 1, 1 - core),
        at(y, z, x + 2, core),
        at(y, z, x + 2, 1 - core),
        at(y, z, x, 1 - core),
        at(y, z + 1, x, core),
        at(y, z - 1, x, core),
        at(y, z - 1 + 2 * core, x, 1 - core),
        at(y + 1, z, x, core),
        at(y - 1, z, x, core),
    ]


def iota(shape, axis):
    return lax.broadcasted_iota(jnp.int32, shape, axis)


def ones_where(hit):
    return jnp.where(hit, 1.0, 0.0).astype(jnp.bfloat16)


def exact(pick, rows):
    return jnp.dot(pick, rows, preferred_element_type=jnp.float32)


def lay_out(index, source, cells):
    owner, frame, row, col, valid = [index[pl.ds(i, 1), :] for i in range(5)]
    one, other = iota((64, 64), 0), iota((64, 64), 1)

    def column(line):
        return jnp.sum(jnp.where(one == other, line, 0), 1, keepdims=True)

    before = (column(owner) == owner) & (one < other) & (column(valid) != 0)
    rank = jnp.sum(jnp.where(before, 1, 0), 0, keepdims=True)
    deep = (owner & 15) >> 1
    spot = jnp.where(deep < 4, 2 * deep + 1, 2 * (7 - deep))
    slot = (((owner >> 4) * 2 + (owner & 1)) * 8 + spot) * 2 + rank
    slot = jnp.where(valid != 0, slot, 999)
    hit = column(slot) == iota((64, 128), 1)
    source[...] = 64 + jnp.sum(jnp.where(hit, iota((64, 128), 0) - 64, 0), 0, keepdims=True)
    base = frame * 256 + row * 16 + col
    bases = [
        jnp.sum(jnp.where(slot == one * 2 + i, base, 0), 1, keepdims=True) for i in range(2)
    ]
    where = iota((64, 128), 1)
    offset = (where & 63) // 8 * 16 + (where & 7)
    cells[...] = (offset + jnp.where(where < 64, bases[0], bases[1])).reshape(8, 8, 128)


def widen(halo, wide, frames, far_there):
    _, _, x, _ = place()
    strip = lax.axis_index("wa")
    cell, other = iota((288, 288), 0), iota((288, 288), 1)
    back = ones_where((other == cell - 1) & (cell % 16 != 0))
    ahead = ones_where((other == cell + 1) & (cell % 16 != 15))
    cell, other = iota((288, 32), 0), iota((288, 32), 1)
    from_left = ones_where(cell == other * 16 + jnp.where(strip > 0, 0, 4096))
    from_right = ones_where(cell == other * 16 + 15 + jnp.where(strip < 15, 0, 4096))
    row = iota((288, 256), 0) // 16
    low, high = jnp.where(x > 0, 0, 1), jnp.where(x < 3, 17, 16)
    for frame in frames:
        far = halo.other <= frame < halo.other + 2
        least = jnp.where(far_there, low, 99) if far else low
        there = (row >= least) & (row <= high)
        flat = halo.ext[frame].reshape(288, 256)
        parts = (
            exact(back, flat) + exact(from_left, halo.left[frame]),
            flat.astype(jnp.float32),
            exact(ahead, flat) + exact(from_right, halo.right[frame]),
        )
        for shift, value in enumerate(parts):
            wide[frame, :, :, 256 * shift : 256 * shift + 256] = (
                jnp.where(there, value, 0.0).astype(jnp.bfloat16).reshape(18, 16, 256)
            )


NT = (((1,), (1,)), ((), ()))


def conv_part(wide, taps, acc, a, first, count, out):
    summed = jnp.zeros((count * 256, 256), jnp.float32)
    for b in range(3):
        at_row = (a * 3 + b) * 768
        summed += jnp.dot(
            wide[first : first + count, b : b + 16].reshape(count * 256, 768),
            taps[at_row : at_row + 768],
            preferred_element_type=jnp.float32,
        )
    acc[out * 256 : (out + count) * 256] += summed


def back_part(wide, taps, acc, a, first, count, out):
    summed = jnp.zeros((count * 256, 256), jnp.float32)
    for b in range(3):
        for c in range(3):
            at_row = ((a * 3 + b) * 3 + c) * 256
            lanes = slice(256 * (2 - c), 256 * (3 - c))
            summed += lax.dot_general(
                wide[first : first + count, 2 - b : 18 - b, :, lanes].reshape(count * 256, 256),
                taps[at_row : at_row + 256],
                NT,
                preferred_element_type=jnp.float32,
            )
    acc[out * 256 : (out + count) * 256] += summed


def middle(preact, tile, down, reduced, grad_pre, acc):
    sig = jax.nn.sigmoid(preact)
    section = (tile[...].reshape(512, 256).astype(jnp.float32) + preact * sig).astype(jnp.bfloat16)
    small, large = iota((128, 512), 0), iota((128, 512), 1)
    first = small // 64 * 256 + small // 8 % 8 * 32 + small % 8 * 2
    pooled = [
        exact(ones_where(large == first + p * 16 + q), section).astype(jnp.bfloat16)
        for p in range(2)
        for q in range(2)
    ]
    reduced[...] = jnp.dot(
        jnp.concatenate(pooled, 1), down[...].reshape(1024, 256), preferred_element_type=jnp.float32
    ).astype(jnp.bfloat16)
    spread = acc[...]
    grad_pre[...] = (spread * sig * (1.0 + preact * (1.0 - sig))).astype(jnp.bfloat16).reshape(
        2, 16, 16, 256
    )


def spread_out(down, grad_out, acc):
    large, small = iota((512, 128), 0), iota((512, 128), 1)
    over = ones_where(small == large // 256 * 64 + large // 32 % 8 * 8 + large // 2 % 8)
    repeated = exact(over, grad_out[...]).astype(jnp.bfloat16)
    cell = iota((512, 256), 0)
    kind = cell // 16 % 2 * 2 + cell % 2
    back = jnp.zeros((512, 256), jnp.float32)
    for which in range(4):
        back = jnp.where(
            kind == which,
            lax.dot_general(repeated, down[which], NT, preferred_element_type=jnp.float32),
            back,
        )
    acc[...] = back


def step_kernel(
    features, weight, indices, crop_grad, down_all, grad_all, reduced, grad_in,
    tile, index, down, grad_out, table, source, cells,
    ext, left, right, edge, ext_b, left_b, right_b, edge_b, grad_pre,
    wide, taps, preact, acc, crop, packed, crops, places, part,
    in_up, in_down, out_up, out_down,
    send_sems, recv_sems, local_sems, up_send, up_recv, down_send, down_recv,
):
    y, z, x, core = place()
    strip = z % 8
    mine = x * 2 + core
    slab = lax.axis_index("ta")
    copies = Copies(send_sems, recv_sems)

    def lane(offset):
        return pl.ds(pl.multiple_of((((strip + offset + 8) % 8) * 2 + core) * 432, 16), 432)

    loads = [
        pltpu.make_async_copy(src, dst, local_sems.at[i])
        for i, (src, dst) in enumerate(
            (
                (indices, index),
                (crop_grad, crop.at[pl.ds(0, 64)]),
                (features, tile),
                (weight, taps.at[lane(0)]),
                (down_all, down),
                (grad_all, grad_out),
            )
        )
    ]
    for load in loads:
        load.start()
    met = greet(partners())
    crop[64] = jnp.zeros_like(crop[64])
    loads[0].wait()
    lay_out(index, table, cells)
    to_scalars = pltpu.make_async_copy(table, source, local_sems.at[6])
    to_scalars.start()
    places[mine] = cells[mine]
    loads[2].wait()
    ext[2:4, 1:17] = tile[...]
    loads[1].wait()
    to_scalars.wait()

    near = [
        (away, flip, ((x + away + 4) % 4) * 2 + (core + flip) % 2)
        for away in (2, 1, -1)
        for flip in range(2)
    ] + [(0, 1, x * 2 + 1 - core)]

    def pack(dest):
        def fill(i, _):
            packed[dest, i // 4, i // 2 % 2, pl.ds(i % 2 * 64, 64)] = crop[source[0, dest * 16 + i]]
            return 0

        lax.fori_loop(0, 16, fill, 0)

    for _, _, dest in near:
        pack(dest)

    def keep(i, _):
        crops[i // 4, i // 2 % 2, mine, pl.ds(i % 2 * 64, 64)] = crop[source[0, mine * 16 + i]]
        return 0

    lax.fori_loop(0, 16, keep, 0)
    for load in loads[3:]:
        load.wait()
    halo = Halo(copies, tile, ext, left, right, edge, 2, 1)
    back = Halo(copies, grad_pre, ext_b, left_b, right_b, edge_b, 0, -1)
    half = pl.ds(pl.multiple_of((y % 2) * 128, 128), 128)
    turn = 1 - 2 * core

    def crops_send(group):
        return [
            copies.start(
                packed.at[dest, group],
                crops.at[group, :, mine],
                at(y, z, x + away, (core + flip) % 2),
            )
            for away, flip, dest in near
        ]

    met()
    arriving, ring, swaps = {}, {}, {}
    halo.send_far(0)
    halo.send_far(1)
    for way in (1, -1):
        piece = taps.at[lane(0), half]
        ring[way] = copies.start(piece, piece, at(y, z + way, x, core))
    halo.own_rows()
    marks = [
        copies.start(cells.at[dest], places.at[mine], at(y, z, x + away, (core + flip) % 2))
        for away, flip, dest in near
    ]
    arriving[0] = crops_send(0)
    halo.send_far(2)
    rest = [copies.start(taps.at[lane(0)], taps.at[lane(0)], at(y, z, x, 1 - core))]

    def swap(offset, y_to):
        piece = taps.at[lane(offset), half]
        swaps[offset] = copies.start(piece, piece, at(y_to, z, x, core))

    def ring_step(step):
        for way in (1, -1):
            ring[way].wait_recv()
            offset = -way * step
            if step < 3:
                piece = taps.at[lane(offset), half]
                ring[way] = copies.start(piece, piece, at(y, z + way, x, core))
            swap(offset, y + way)

    def whole(offset):
        swaps[offset].wait_recv()
        shard_all = taps.at[lane(offset)]
        rest.append(copies.start(shard_all, shard_all, at(y, z, x, 1 - core)))

    cell = iota((512, 128), 0)

    def settle(group):
        for copy in arriving[group] + (marks if group == 0 else []):
            copy.wait_recv()
        for i in range(2):
            goal = 7 - group if i == 0 else group
            part[goal] = jnp.zeros_like(part[goal])

            def add(pair, _):
                hits = [
                    ones_where(cell == places[2 * pair + j, 2 * group + i][None, :])
                    for j in range(2)
                ]
                part[goal] += jnp.dot(
                    jnp.concatenate(hits, 1),
                    crops[group, i, pl.ds(2 * pair, 2)].reshape(256, 256),
                    preferred_element_type=jnp.float32,
                )
                return 0

            lax.fori_loop(0, 4, add, 0)

    def chain(goal, chunk, way):
        landing, leaving, sends, recvs = (
            (in_up, out_up, up_send, up_recv) if way == 1 else (in_down, out_down, down_send, down_recv)
        )
        return pltpu.make_async_remote_copy(
            src_ref=leaving.at[goal, chunk],
            dst_ref=landing.at[goal, chunk],
            send_sem=sends.at[goal, chunk],
            recv_sem=recvs.at[goal, chunk],
            device_id=at(y, z + way, x, core),
            device_id_type=MESH,
        )

    def turn_of(step, way):
        rank = strip if way == 1 else 7 - strip
        turn_at = step - rank + 16
        late = (turn_at - 16 + 32) % 32
        odd = late % 2
        ahead = (1 - odd) * (7 - late // 2) + odd * (late // 2)
        busy = (late < 8) & (late != 1) & (rank < ahead)
        return rank, (ahead if way == 1 else 7 - ahead), busy

    def advance(step, chunk, way):
        rank, goal, busy = turn_of(step, way)
        landing, leaving = (in_up, out_up) if way == 1 else (in_down, out_down)

        @pl.when(busy)
        def _():
            copy = chain(goal, chunk, way)
            mid = part[goal, pl.ds(chunk * 256, 256)]

            @pl.when(rank > 0)
            def _():
                copy.wait_recv()
                leaving[goal, chunk] = (mid + landing[goal, chunk].astype(jnp.float32)).astype(
                    jnp.bfloat16
                )

            @pl.when(rank == 0)
            def _():
                leaving[goal, chunk] = mid.astype(jnp.bfloat16)

            copy.start()

    def slot(step):
        for chunk in range(2):
            for way in (1, -1):
                advance(step, chunk, way)

    ring_step(1)
    halo.send_far(3)
    halo.far_rows()
    arriving[1] = crops_send(1)
    halo.near_columns()
    ring_step(2)
    halo.send_far(4)
    spread_out(down, grad_out, acc)
    settle(0)
    slot(0)
    arriving[2] = crops_send(2)
    ring_step(3)
    piece = taps.at[lane(-3 * turn), half]
    ring_last = copies.start(piece, piece, at(y, z + turn, x, core))
    for offset in (1, -1, 2, -2):
        whole(offset)
    slot(1)
    ring_last.wait_recv()
    swap(4, y + turn)
    settle(1)
    slot(2)
    arriving[3] = crops_send(3)
    for offset in (3, -3, 4):
        whole(offset)
    for copy in halo.near_sides + rest:
        copy.wait_recv()
    preact[...] = jnp.zeros_like(preact)
    widen(halo, wide, (2, 3), slab > 0)
    conv_part(wide, taps, preact, 2, 2, 2, 0)
    slot(3)
    conv_part(wide, taps, preact, 1, 2, 1, 1)
    halo.far_columns()
    settle(2)
    slot(4)
    for copy in halo.far_sides:
        copy.wait_recv()
    widen(halo, wide, (0, 1), slab > 0)
    conv_part(wide, taps, preact, 0, 0, 2, 0)
    conv_part(wide, taps, preact, 1, 1, 1, 0)
    middle(preact[...], tile, down, reduced, grad_pre, acc)
    back.send_far(0)
    back.send_far(1)
    back.own_rows()
    back.send_far(2)
    ext_b[0:2, 1:17] = grad_pre[...]
    slot(5)
    back.send_far(3)
    settle(3)
    slot(6)
    back.near_columns()
    back.send_far(4)
    slot(7)
    back.far_rows()
    slot(8)
    for copy in back.near_sides:
        copy.wait_recv()
    widen(back, wide, (0, 1), slab < 7)
    slot(9)
    back_part(wide, taps, acc, 2, 0, 2, 0)
    back_part(wide, taps, acc, 1, 1, 1, 0)
    back.far_columns()
    assert copies.used == SENDS, copies.used
    for chunk in range(2):
        place_at = pl.ds(chunk * 256, 256)
        acc[place_at] += part[strip, place_at]
        for way in (1, -1):
            landing = in_up if way == 1 else in_down

            @pl.when((strip if way == 1 else 7 - strip) > 0)
            def _():
                chain(strip, chunk, way).wait_recv()
                acc[place_at] += landing[strip, chunk].astype(jnp.float32)

    for copy in back.far_sides:
        copy.wait_recv()
    widen(back, wide, (2, 3), slab < 7)
    back_part(wide, taps, acc, 0, 2, 2, 0)
    back_part(wide, taps, acc, 1, 2, 1, 1)
    grad_in[...] = acc[...].astype(jnp.bfloat16)
    for step in range(10):
        for chunk in range(2):
            for way in (1, -1):
                rank, goal, busy = turn_of(step, way)

                @pl.when(busy)
                def _():
                    chain(goal, chunk, way).wait_send()

    for copy in copies.sent:
        copy.wait_send()


def hand_on(reduced, grad_in, reduced_out, grad_out):
    reduced_out[...] = reduced[...]
    grad_out[...] = grad_in[...]


SENDS = 93
DMA = pltpu.SemaphoreType.DMA


def per_device(
    features, conv_weight, down_weight, grad_out, crop_grad,
    crop_owner, crop_frame, crop_row, crop_col, crop_valid,
):
    frames, rows, cols, width = features.shape
    half_type, shape, vmem = jnp.bfloat16, jax.ShapeDtypeStruct, pltpu.VMEM
    indices = jnp.stack(
        [crop_owner[:, 0], crop_frame, crop_row, crop_col, crop_valid] + [crop_valid] * 3, 0
    )
    halo = [
        vmem((4, 18, 16, width), half_type), vmem((4, 32, width), half_type),
        vmem((4, 32, width), half_type), vmem((2, 4, 32, width), half_type),
    ]
    tile = vmem((2, 16, 16, width), half_type)
    chain = vmem((8, 2, 256, width), half_type)
    reduced, grad_in = pl.pallas_call(
        step_kernel,
        out_shape=(shape((128, width), half_type), shape((512, width), half_type)),
        in_specs=[pl.BlockSpec(memory_space=pl.ANY)] * 6,
        out_specs=[pl.BlockSpec(memory_space=pltpu.VMEM)] * 2,
        scratch_shapes=[
            tile, vmem((8, 64), jnp.int32), vmem((4, width, width), half_type),
            vmem((128, width), half_type), vmem((1, 128), jnp.int32),
            pltpu.SMEM((1, 128), jnp.int32), vmem((8, 8, 128), jnp.int32),
            *halo, *halo, tile,
            vmem((4, 18, 16, 3 * width), half_type), vmem((6912, width), half_type),
            vmem((512, width), jnp.float32), vmem((512, width), jnp.float32),
            vmem((65, 64, width), half_type), vmem((8, 4, 2, 128, width), half_type),
            vmem((4, 2, 8, 128, width), half_type), vmem((8, 8, 128), jnp.int32),
            vmem((8, 512, width), jnp.float32),
            chain, chain, chain, chain,
            DMA((SENDS,)), DMA((SENDS,)), DMA((7,)),
            DMA((8, 2)), DMA((8, 2)), DMA((8, 2)), DMA((8, 2)),
        ],
        compiler_params=pltpu.CompilerParams(
            collective_id=0, has_side_effects=True, vmem_limit_bytes=60 << 20
        ),
    )(
        features, conv_weight, indices, crop_grad.reshape(64, 64, width),
        down_weight.reshape(4, width, width), grad_out.reshape(-1, width),
    )
    reduced, grad_in = pl.pallas_call(
        hand_on,
        out_shape=(shape((128, width), half_type), shape((512, width), half_type)),
        in_specs=[pl.BlockSpec(memory_space=pltpu.VMEM)] * 2,
        out_specs=[pl.BlockSpec(memory_space=pltpu.VMEM)] * 2,
    )(reduced, grad_in)
    return (
        reduced.reshape(frames, rows // 2, cols // 2, width),
        grad_in.reshape(frames, rows, cols, width),
    )


def solution(mesh):
    spread_all = ("ta", "ha", "wa")
    tile = P("ta", "ha", "wa", None)
    in_specs = (
        tile, P("wa", None), P(), tile, P(spread_all, None, None, None), P(spread_all, None),
        P(spread_all), P(spread_all), P(spread_all), P(spread_all),
    )
    return jax.shard_map(
        per_device, mesh=mesh, in_specs=in_specs, out_specs=(tile, tile), check_vma=False
    )
```

```python
import jax
import jax.numpy as jnp
from jax import lax
from jax.experimental import pallas as pl
from jax.experimental.pallas import tpu as pltpu
from jax.sharding import PartitionSpec as P

MESH = pl.DeviceIdType.MESH
CAP = 2


def place():
    slab, x, strip = lax.axis_index("ta"), lax.axis_index("ha"), lax.axis_index("wa")
    return slab // 2, (slab % 2) * 8 + strip // 2, x, strip % 2


def at(y, z, x, core):
    y, z, x = (y + 4) % 4, (z + 16) % 16, (x + 4) % 4
    return (y * 2 + z // 8, x, (z % 8) * 2 + core)


class Copies:
    def __init__(self, send_sems, recv_sems):
        self.send_sems, self.recv_sems, self.used, self.sent = send_sems, recv_sems, 0, []

    def make(self, src, dst, device):
        slot = self.used
        self.used += 1
        return pltpu.make_async_remote_copy(
            src_ref=src,
            dst_ref=dst,
            send_sem=self.send_sems.at[slot],
            recv_sem=self.recv_sems.at[slot],
            device_id=device,
            device_id_type=MESH,
        )

    def start(self, src, dst, device):
        copy = self.make(src, dst, device)
        copy.start()
        self.sent.append(copy)
        return copy


def greet(devices):
    barrier = pltpu.get_barrier_semaphore()
    for device in devices:
        pl.semaphore_signal(barrier, inc=1, device_id=device, device_id_type=MESH)
    return lambda: pl.semaphore_wait(barrier, len(devices))


def edge_columns(ext, edge, frame):
    rows, cols, width = ext.shape[1:]
    flat = ext[frame].reshape(rows * cols, width)
    row = lax.broadcasted_iota(jnp.int32, (edge.shape[2], rows * cols), 0)
    cell = lax.broadcasted_iota(jnp.int32, (edge.shape[2], rows * cols), 1)
    for side, col in ((0, 0), (1, cols - 1)):
        pick = jnp.where(cell == row * cols + col, 1.0, 0.0).astype(jnp.bfloat16)
        edge[side, frame] = jnp.dot(pick, flat, preferred_element_type=jnp.float32).astype(
            jnp.bfloat16
        )


FAR = ((0, 1), (15, 1), (1, 5), (6, 5), (11, 4))


class Halo:
    def __init__(self, copies, tile, ext, left, right, edge, own, step):
        self.copies, self.tile, self.ext, self.left, self.right = copies, tile, ext, left, right
        self.edge, self.own, self.other, self.step = edge, own, 2 - own, step
        self.far = []

    def send_far(self, piece):
        y, z, x, core = place()
        y_to = y + z // 8 if self.step == 1 else y - 1 + z // 8
        first, count = FAR[piece]
        for frame in range(2):
            self.far.append(
                self.copies.start(
                    self.tile.at[frame, pl.ds(first, count)],
                    self.ext.at[self.other + frame, pl.ds(1 + first, count)],
                    at(y_to, z + 8, x, core),
                )
            )

    def own_rows(self):
        y, z, x, core = place()
        ext, own = self.ext, self.own
        self.rows_own = [
            self.copies.start(
                self.tile.at[:, pl.ds(15, 1)],
                ext.at[pl.ds(own, 2), pl.ds(0, 1)],
                at(y, z, x + 1, core),
            ),
            self.copies.start(
                self.tile.at[:, pl.ds(0, 1)],
                ext.at[pl.ds(own, 2), pl.ds(17, 1)],
                at(y, z, x - 1, core),
            ),
        ]

    def sides(self, first):
        y, z, x, core = place()
        two = pl.ds(first, 2)
        return [
            self.copies.start(
                self.edge.at[1, two], self.left.at[two], at(y, z + core, x, 1 - core)
            ),
            self.copies.start(
                self.edge.at[0, two], self.right.at[two], at(y, z - 1 + core, x, 1 - core)
            ),
        ]

    def near_columns(self):
        for copy in self.rows_own:
            copy.wait_recv()
        for frame in range(2):
            edge_columns(self.ext, self.edge, self.own + frame)
        self.near_sides = self.sides(self.own)

    def far_rows(self):
        y, z, x, core = place()
        ext, two = self.ext, pl.ds(self.other, 2)
        for copy in self.far[:4]:
            copy.wait_recv()
        self.borders = [
            self.copies.start(
                ext.at[two, pl.ds(16, 1)], ext.at[two, pl.ds(0, 1)], at(y, z, x + 1, core)
            ),
            self.copies.start(
                ext.at[two, pl.ds(1, 1)], ext.at[two, pl.ds(17, 1)], at(y, z, x - 1, core)
            ),
        ]

    def far_columns(self):
        for copy in self.far[4:] + self.borders:
            copy.wait_recv()
        for frame in range(2):
            edge_columns(self.ext, self.edge, self.other + frame)
        self.far_sides = self.sides(self.other)


def partners():
    y, z, x, core = place()
    return [
        at(y, z + 8, x, core),
        at(y + 1, z + 8, x, core),
        at(y - 1, z + 8, x, core),
        at(y, z, x + 1, core),
        at(y, z, x - 1, core),
        at(y, z, x + 1, 1 - core),
        at(y, z, x - 1, 1 - core),
        at(y, z, x + 2, core),
        at(y, z, x + 2, 1 - core),
        at(y, z, x, 1 - core),
        at(y, z + 1, x, core),
        at(y, z - 1, x, core),
        at(y, z - 1 + 2 * core, x, 1 - core),
        at(y + 1, z, x, core),
        at(y - 1, z, x, core),
    ]


def iota(shape, axis):
    return lax.broadcasted_iota(jnp.int32, shape, axis)


def ones_where(hit):
    return jnp.where(hit, 1.0, 0.0).astype(jnp.bfloat16)


def exact(pick, rows):
    return jnp.dot(pick, rows, preferred_element_type=jnp.float32)


def lay_out(index, source, cells):
    owner, frame, row, col, valid = [index[pl.ds(i, 1), :] for i in range(5)]
    one, other = iota((64, 64), 0), iota((64, 64), 1)

    def column(line):
        return jnp.sum(jnp.where(one == other, line, 0), 1, keepdims=True)

    before = (column(owner) == owner) & (one < other) & (column(valid) != 0)
    rank = jnp.sum(jnp.where(before, 1, 0), 0, keepdims=True)
    deep = (owner & 15) >> 1
    spot = jnp.where(deep < 4, 2 * deep + 1, 2 * (7 - deep))
    slot = (((owner >> 4) * 2 + (owner & 1)) * 8 + spot) * 2 + rank
    slot = jnp.where(valid != 0, slot, 999)
    hit = column(slot) == iota((64, 128), 1)
    source[...] = 64 + jnp.sum(jnp.where(hit, iota((64, 128), 0) - 64, 0), 0, keepdims=True)
    base = frame * 256 + row * 16 + col
    bases = [
        jnp.sum(jnp.where(slot == one * 2 + i, base, 0), 1, keepdims=True) for i in range(2)
    ]
    where = iota((64, 128), 1)
    offset = (where & 63) // 8 * 16 + (where & 7)
    cells[...] = (offset + jnp.where(where < 64, bases[0], bases[1])).reshape(8, 8, 128)


def widen(halo, wide, frames, far_there):
    _, _, x, _ = place()
    strip = lax.axis_index("wa")
    cell, other = iota((288, 288), 0), iota((288, 288), 1)
    back = ones_where((other == cell - 1) & (cell % 16 != 0))
    ahead = ones_where((other == cell + 1) & (cell % 16 != 15))
    cell, other = iota((288, 32), 0), iota((288, 32), 1)
    from_left = ones_where(cell == other * 16 + jnp.where(strip > 0, 0, 4096))
    from_right = ones_where(cell == other * 16 + 15 + jnp.where(strip < 15, 0, 4096))
    row = iota((288, 256), 0) // 16
    low, high = jnp.where(x > 0, 0, 1), jnp.where(x < 3, 17, 16)
    for frame in frames:
        far = halo.other <= frame < halo.other + 2
        least = jnp.where(far_there, low, 99) if far else low
        there = (row >= least) & (row <= high)
        flat = halo.ext[frame].reshape(288, 256)
        parts = (
            exact(back, flat) + exact(from_left, halo.left[frame]),
            flat.astype(jnp.float32),
            exact(ahead, flat) + exact(from_right, halo.right[frame]),
        )
        for shift, value in enumerate(parts):
            wide[frame, :, :, 256 * shift : 256 * shift + 256] = (
                jnp.where(there, value, 0.0).astype(jnp.bfloat16).reshape(18, 16, 256)
            )


NT = (((1,), (1,)), ((), ()))


def conv_part(wide, taps, acc, a, first, count, out):
    summed = jnp.zeros((count * 256, 256), jnp.float32)
    for b in range(3):
        at_row = (a * 3 + b) * 768
        summed += jnp.dot(
            wide[first : first + count, b : b + 16].reshape(count * 256, 768),
            taps[at_row : at_row + 768],
            preferred_element_type=jnp.float32,
        )
    acc[out * 256 : (out + count) * 256] += summed


def back_part(wide, taps, acc, a, first, count, out):
    summed = jnp.zeros((count * 256, 256), jnp.float32)
    for b in range(3):
        for c in range(3):
            at_row = ((a * 3 + b) * 3 + c) * 256
            lanes = slice(256 * (2 - c), 256 * (3 - c))
            summed += lax.dot_general(
                wide[first : first + count, 2 - b : 18 - b, :, lanes].reshape(count * 256, 256),
                taps[at_row : at_row + 256],
                NT,
                preferred_element_type=jnp.float32,
            )
    acc[out * 256 : (out + count) * 256] += summed


def middle(preact, tile, down, reduced, grad_pre, acc):
    sig = jax.nn.sigmoid(preact)
    section = (tile[...].reshape(512, 256).astype(jnp.float32) + preact * sig).astype(jnp.bfloat16)
    small, large = iota((128, 512), 0), iota((128, 512), 1)
    first = small // 64 * 256 + small // 8 % 8 * 32 + small % 8 * 2
    pooled = [
        exact(ones_where(large == first + p * 16 + q), section).astype(jnp.bfloat16)
        for p in range(2)
        for q in range(2)
    ]
    reduced[...] = jnp.dot(
        jnp.concatenate(pooled, 1), down[...].reshape(1024, 256), preferred_element_type=jnp.float32
    ).astype(jnp.bfloat16)
    spread = acc[...]
    grad_pre[...] = (spread * sig * (1.0 + preact * (1.0 - sig))).astype(jnp.bfloat16).reshape(
        2, 16, 16, 256
    )


def spread_out(down, grad_out, acc):
    large, small = iota((512, 128), 0), iota((512, 128), 1)
    over = ones_where(small == large // 256 * 64 + large // 32 % 8 * 8 + large // 2 % 8)
    repeated = exact(over, grad_out[...]).astype(jnp.bfloat16)
    cell = iota((512, 256), 0)
    kind = cell // 16 % 2 * 2 + cell % 2
    back = jnp.zeros((512, 256), jnp.float32)
    for which in range(4):
        back = jnp.where(
            kind == which,
            lax.dot_general(repeated, down[which], NT, preferred_element_type=jnp.float32),
            back,
        )
    acc[...] = back


def step_kernel(
    features, weight, indices, crop_grad, down_all, grad_all, reduced, grad_in,
    tile, index, down, grad_out, table, source, cells,
    ext, left, right, edge, ext_b, left_b, right_b, edge_b, grad_pre,
    wide, taps, preact, acc, crop, packed, crops, places, part,
    in_up, in_down, out_up, out_down,
    send_sems, recv_sems, local_sems, up_send, up_recv, down_send, down_recv,
):
    y, z, x, core = place()
    strip = z % 8
    mine = x * 2 + core
    slab = lax.axis_index("ta")
    copies = Copies(send_sems, recv_sems)

    def lane(offset):
        return pl.ds(pl.multiple_of((((strip + offset + 8) % 8) * 2 + core) * 432, 16), 432)

    loads = [
        pltpu.make_async_copy(src, dst, local_sems.at[i])
        for i, (src, dst) in enumerate(
            (
                (indices, index),
                (crop_grad, crop.at[pl.ds(0, 64)]),
                (features, tile),
                (weight, taps.at[lane(0)]),
                (down_all, down),
                (grad_all, grad_out),
            )
        )
    ]
    for load in loads:
        load.start()
    met = greet(partners())
    crop[64] = jnp.zeros_like(crop[64])
    loads[0].wait()
    lay_out(index, table, cells)
    to_scalars = pltpu.make_async_copy(table, source, local_sems.at[6])
    to_scalars.start()
    places[mine] = cells[mine]
    loads[2].wait()
    ext[2:4, 1:17] = tile[...]
    loads[1].wait()
    to_scalars.wait()

    near = [
        (away, flip, ((x + away + 4) % 4) * 2 + (core + flip) % 2)
        for away in (2, 1, -1)
        for flip in range(2)
    ] + [(0, 1, x * 2 + 1 - core)]

    def pack(dest):
        def fill(i, _):
            packed[dest, i // 4, i // 2 % 2, pl.ds(i % 2 * 64, 64)] = crop[source[0, dest * 16 + i]]
            return 0

        lax.fori_loop(0, 16, fill, 0)

    for _, _, dest in near:
        pack(dest)

    def keep(i, _):
        crops[i // 4, i // 2 % 2, mine, pl.ds(i % 2 * 64, 64)] = crop[source[0, mine * 16 + i]]
        return 0

    lax.fori_loop(0, 16, keep, 0)
    for load in loads[3:]:
        load.wait()
    halo = Halo(copies, tile, ext, left, right, edge, 2, 1)
    back = Halo(copies, grad_pre, ext_b, left_b, right_b, edge_b, 0, -1)
    half = pl.ds(pl.multiple_of((y % 2) * 128, 128), 128)
    turn = 1 - 2 * core

    def crops_send(group):
        return [
            copies.start(
                packed.at[dest, group],
                crops.at[group, :, mine],
                at(y, z, x + away, (core + flip) % 2),
            )
            for away, flip, dest in near
        ]

    met()
    arriving, ring, swaps = {}, {}, {}
    halo.send_far(0)
    halo.send_far(1)
    for way in (1, -1):
        piece = taps.at[lane(0), half]
        ring[way] = copies.start(piece, piece, at(y, z + way, x, core))
    halo.own_rows()
    marks = [
        copies.start(cells.at[dest], places.at[mine], at(y, z, x + away, (core + flip) % 2))
        for away, flip, dest in near
    ]
    arriving[0] = crops_send(0)
    halo.send_far(2)
    rest = [copies.start(taps.at[lane(0)], taps.at[lane(0)], at(y, z, x, 1 - core))]

    def swap(offset, y_to):
        piece = taps.at[lane(offset), half]
        swaps[offset] = copies.start(piece, piece, at(y_to, z, x, core))

    def ring_step(step):
        for way in (1, -1):
            ring[way].wait_recv()
            offset = -way * step
            if step < 3:
                piece = taps.at[lane(offset), half]
                ring[way] = copies.start(piece, piece, at(y, z + way, x, core))
            swap(offset, y + way)

    def whole(offset):
        swaps[offset].wait_recv()
        shard_all = taps.at[lane(offset)]
        rest.append(copies.start(shard_all, shard_all, at(y, z, x, 1 - core)))

    cell = iota((512, 128), 0)

    def settle(group):
        for copy in arriving[group] + (marks if group == 0 else []):
            copy.wait_recv()
        for i in range(2):
            goal = 7 - group if i == 0 else group
            part[goal] = jnp.zeros_like(part[goal])

            def add(pair, _):
                hits = [
                    ones_where(cell == places[2 * pair + j, 2 * group + i][None, :])
                    for j in range(2)
                ]
                part[goal] += jnp.dot(
                    jnp.concatenate(hits, 1),
                    crops[group, i, pl.ds(2 * pair, 2)].reshape(256, 256),
                    preferred_element_type=jnp.float32,
                )
                return 0

            lax.fori_loop(0, 4, add, 0)

    def chain(goal, chunk, way):
        landing, leaving, sends, recvs = (
            (in_up, out_up, up_send, up_recv) if way == 1 else (in_down, out_down, down_send, down_recv)
        )
        return pltpu.make_async_remote_copy(
            src_ref=leaving.at[goal, chunk],
            dst_ref=landing.at[goal, chunk],
            send_sem=sends.at[goal, chunk],
            recv_sem=recvs.at[goal, chunk],
            device_id=at(y, z + way, x, core),
            device_id_type=MESH,
        )

    def turn_of(step, way):
        rank = strip if way == 1 else 7 - strip
        turn_at = step - rank + 16
        late = (turn_at - 16 + 32) % 32
        odd = late % 2
        ahead = (1 - odd) * (7 - late // 2) + odd * (late // 2)
        busy = (late < 8) & (late != 1) & (rank < ahead)
        return rank, (ahead if way == 1 else 7 - ahead), busy

    def advance(step, chunk, way):
        rank, goal, busy = turn_of(step, way)
        landing, leaving = (in_up, out_up) if way == 1 else (in_down, out_down)

        @pl.when(busy)
        def _():
            copy = chain(goal, chunk, way)
            mid = part[goal, pl.ds(chunk * 256, 256)]

            @pl.when(rank > 0)
            def _():
                copy.wait_recv()
                leaving[goal, chunk] = (mid + landing[goal, chunk].astype(jnp.float32)).astype(
                    jnp.bfloat16
                )

            @pl.when(rank == 0)
            def _():
                leaving[goal, chunk] = mid.astype(jnp.bfloat16)

            copy.start()

    def slot(step):
        for chunk in range(2):
            for way in (1, -1):
                advance(step, chunk, way)

    ring_step(1)
    halo.send_far(3)
    halo.far_rows()
    arriving[1] = crops_send(1)
    halo.near_columns()
    ring_step(2)
    halo.send_far(4)
    spread_out(down, grad_out, acc)
    settle(0)
    slot(0)
    arriving[2] = crops_send(2)
    ring_step(3)
    piece = taps.at[lane(-3 * turn), half]
    ring_last = copies.start(piece, piece, at(y, z + turn, x, core))
    for offset in (1, -1, 2, -2):
        whole(offset)
    slot(1)
    ring_last.wait_recv()
    swap(4, y + turn)
    settle(1)
    slot(2)
    arriving[3] = crops_send(3)
    for offset in (3, -3, 4):
        whole(offset)
    for copy in halo.near_sides + rest:
        copy.wait_recv()
    preact[...] = jnp.zeros_like(preact)
    widen(halo, wide, (2, 3), slab > 0)
    conv_part(wide, taps, preact, 2, 2, 2, 0)
    slot(3)
    conv_part(wide, taps, preact, 1, 2, 1, 1)
    halo.far_columns()
    settle(2)
    slot(4)
    for copy in halo.far_sides:
        copy.wait_recv()
    widen(halo, wide, (0, 1), slab > 0)
    conv_part(wide, taps, preact, 0, 0, 2, 0)
    conv_part(wide, taps, preact, 1, 1, 1, 0)
    middle(preact[...], tile, down, reduced, grad_pre, acc)
    back.send_far(0)
    back.send_far(1)
    back.own_rows()
    back.send_far(2)
    back.send_far(3)
    ext_b[0:2, 1:17] = grad_pre[...]
    slot(5)
    back.send_far(4)
    settle(3)
    slot(6)
    back.near_columns()
    slot(7)
    back.far_rows()
    slot(8)
    for copy in back.near_sides:
        copy.wait_recv()
    widen(back, wide, (0, 1), slab < 7)
    slot(9)
    back_part(wide, taps, acc, 2, 0, 2, 0)
    back_part(wide, taps, acc, 1, 1, 1, 0)
    back.far_columns()
    assert copies.used == SENDS, copies.used
    for chunk in range(2):
        place_at = pl.ds(chunk * 256, 256)
        acc[place_at] += part[strip, place_at]
        for way in (1, -1):
            landing = in_up if way == 1 else in_down

            @pl.when((strip if way == 1 else 7 - strip) > 0)
            def _():
                chain(strip, chunk, way).wait_recv()
                acc[place_at] += landing[strip, chunk].astype(jnp.float32)

    for copy in back.far_sides:
        copy.wait_recv()
    widen(back, wide, (2, 3), slab < 7)
    back_part(wide, taps, acc, 0, 2, 2, 0)
    back_part(wide, taps, acc, 1, 2, 1, 1)
    grad_in[...] = acc[...].astype(jnp.bfloat16)
    for step in range(10):
        for chunk in range(2):
            for way in (1, -1):
                rank, goal, busy = turn_of(step, way)

                @pl.when(busy)
                def _():
                    chain(goal, chunk, way).wait_send()

    for copy in copies.sent:
        copy.wait_send()


def hand_on(reduced, grad_in, reduced_out, grad_out):
    reduced_out[...] = reduced[...]
    grad_out[...] = grad_in[...]


SENDS = 93
DMA = pltpu.SemaphoreType.DMA


def per_device(
    features, conv_weight, down_weight, grad_out, crop_grad,
    crop_owner, crop_frame, crop_row, crop_col, crop_valid,
):
    frames, rows, cols, width = features.shape
    half_type, shape, vmem = jnp.bfloat16, jax.ShapeDtypeStruct, pltpu.VMEM
    indices = jnp.stack(
        [crop_owner[:, 0], crop_frame, crop_row, crop_col, crop_valid] + [crop_valid] * 3, 0
    )
    halo = [
        vmem((4, 18, 16, width), half_type), vmem((4, 32, width), half_type),
        vmem((4, 32, width), half_type), vmem((2, 4, 32, width), half_type),
    ]
    tile = vmem((2, 16, 16, width), half_type)
    chain = vmem((8, 2, 256, width), half_type)
    reduced, grad_in = pl.pallas_call(
        step_kernel,
        out_shape=(shape((128, width), half_type), shape((512, width), half_type)),
        in_specs=[pl.BlockSpec(memory_space=pl.ANY)] * 6,
        out_specs=[pl.BlockSpec(memory_space=pltpu.VMEM)] * 2,
        scratch_shapes=[
            tile, vmem((8, 64), jnp.int32), vmem((4, width, width), half_type),
            vmem((128, width), half_type), vmem((1, 128), jnp.int32),
            pltpu.SMEM((1, 128), jnp.int32), vmem((8, 8, 128), jnp.int32),
            *halo, *halo, tile,
            vmem((4, 18, 16, 3 * width), half_type), vmem((6912, width), half_type),
            vmem((512, width), jnp.float32), vmem((512, width), jnp.float32),
            vmem((65, 64, width), half_type), vmem((8, 4, 2, 128, width), half_type),
            vmem((4, 2, 8, 128, width), half_type), vmem((8, 8, 128), jnp.int32),
            vmem((8, 512, width), jnp.float32),
            chain, chain, chain, chain,
            DMA((SENDS,)), DMA((SENDS,)), DMA((7,)),
            DMA((8, 2)), DMA((8, 2)), DMA((8, 2)), DMA((8, 2)),
        ],
        compiler_params=pltpu.CompilerParams(
            collective_id=0, has_side_effects=True, vmem_limit_bytes=60 << 20
        ),
    )(
        features, conv_weight, indices, crop_grad.reshape(64, 64, width),
        down_weight.reshape(4, width, width), grad_out.reshape(-1, width),
    )
    reduced, grad_in = pl.pallas_call(
        hand_on,
        out_shape=(shape((128, width), half_type), shape((512, width), half_type)),
        in_specs=[pl.BlockSpec(memory_space=pltpu.VMEM)] * 2,
        out_specs=[pl.BlockSpec(memory_space=pltpu.VMEM)] * 2,
    )(reduced, grad_in)
    return (
        reduced.reshape(frames, rows // 2, cols // 2, width),
        grad_in.reshape(frames, rows, cols, width),
    )


def solution(mesh):
    spread_all = ("ta", "ha", "wa")
    tile = P("ta", "ha", "wa", None)
    in_specs = (
        tile, P("wa", None), P(), tile, P(spread_all, None, None, None), P(spread_all, None),
        P(spread_all), P(spread_all), P(spread_all), P(spread_all),
    )
    return jax.shard_map(
        per_device, mesh=mesh, in_specs=in_specs, out_specs=(tile, tile), check_vma=False
    )
```
